512 devices in a mesh: clusters: 32 (over z, core), group: 16 (over x, y).
Axes of the slice: x: 4, y: 4, z: 16, core: 2. Of those that a mesh axis runs over, the one named last changes fastest.
Arguments:
- embeddings: bfloat16 [262144, 1024], P(('clusters', 'group')), may hold values from -20 to 20
- new_label: int32 [262144], P(('clusters', 'group')), may hold values from 0 to 31, as said below
- dest_member: int32 [262144], P(('clusters', 'group')), may hold values from 0 to 15, as said below
- seed_index: int32 [32, 512], P('clusters'), may hold values from 0 to 8191, as said below
- kappa: float32 [32], P('clusters'), may hold values from 8 to 400
Outputs:
- centroids: bfloat16 [16384, 1024], P('clusters')
- row_score: float32 [524288], P(('clusters', 'group'))
The draws below stay inside these ranges and needn't reach their ends.
Inputs may be any that keep to these rules, and one draw needn't show every extreme that they name: `new_label`: each device sends between 192 and 320 of its rows to devices of other coarse clusters, at most 1 to any one device; in every draw one device receives exactly 1 row from every device of the other clusters, and every device sends exactly 1 row to some device. Rows whose label is their own device's cluster stay. `dest_member`: A row whose new_label is its own device's cluster has its own device's index along group here. `seed_index`: the 512 entries of cluster c are distinct positions m * 512 + s among the rows held before the move by cluster c's devices (m along group, s the row on that device), each naming a row whose new_label is c.
All inputs are finite; a program needn't handle non-finite values.
Results may differ from the reference program's by a relative error of at most 0.02.
The reference program's roundings to bfloat16 on the way count: a program that leaves them out, or rounds other values in their place, can miss the bound.
Values may be sent and summed in bfloat16 or wider, within the bound.
A program may use at most 64 MiB of HBM per device.

```python
import jax
import jax.numpy as jnp
from jax import lax

D = 1024
K = 512
ROWS = 512
ITERS = 2
COARSE = 32
MEMBERS = 16
CAP = 1
SLOTS = 1024
TOTAL = 262144


def route_plan(key):
    devices = COARSE * MEMBERS
    slot_total = devices * CAP
    movers_least = ROWS * 3 // 8
    movers_most = ROWS * 5 // 8
    base_key = jax.random.fold_in(key, 11)
    popular = jax.random.randint(jax.random.fold_in(base_key, 1), (COARSE,), 0, 4)
    hot_cluster = jax.random.randint(jax.random.fold_in(base_key, 2), (), 0, COARSE)
    hot_member = jax.random.randint(jax.random.fold_in(base_key, 3), (), 0, MEMBERS)
    spare_member = jax.random.randint(jax.random.fold_in(base_key, 4), (), 0, MEMBERS)

    def device_plan(anchor):
        device_key = jax.random.fold_in(base_key, anchor + 100)
        key_noise, key_count, key_order = jax.random.split(device_key, 3)
        home = anchor // MEMBERS
        member = anchor % MEMBERS
        slot_ids = jnp.arange(slot_total, dtype=jnp.int32)
        target = slot_ids // CAP
        target_cluster = target // MEMBERS
        jitter = jax.random.randint(key_noise, (slot_total,), 0, 1024)
        priority = jitter + 300 * popular[target_cluster]
        forced = jnp.where(home == hot_cluster, (hot_cluster + 1) % COARSE * MEMBERS + spare_member, hot_cluster * MEMBERS + hot_member)
        priority = jnp.where(target == forced, 4000, priority)
        priority = jnp.where(target_cluster == home, -1, priority)
        ranked = jnp.argsort(-(priority * slot_total + slot_ids))
        count = jax.random.randint(key_count, (), movers_least, movers_most + 1)
        chosen = ranked[:movers_most] // CAP
        active = jnp.arange(movers_most) < count
        shuffled = jax.random.permutation(key_order, ROWS)[:movers_most]
        labels = jnp.full((ROWS,), home, jnp.int32).at[shuffled].set(jnp.where(active, chosen // MEMBERS, home).astype(jnp.int32))
        members = jnp.full((ROWS,), member, jnp.int32).at[shuffled].set(jnp.where(active, chosen % MEMBERS, member).astype(jnp.int32))
        return (labels, members)
    labels, members = jax.vmap(device_plan)(jnp.arange(devices, dtype=jnp.int32))
    return (labels.reshape(-1), members.reshape(-1))


def draw_new_label(key, part):
    return route_plan(key)[0]


def draw_dest_member(key, part):
    return route_plan(key)[1]


def draw_seed_index(key, part):
    labels = route_plan(key)[0]
    span = MEMBERS * ROWS

    def cluster_seeds(cluster):
        held = lax.dynamic_slice_in_dim(labels, cluster * span, span)
        stays = (held == cluster).astype(jnp.int32)
        shuffled = jax.random.permutation(jax.random.fold_in(key, 500 + cluster), span).astype(jnp.int32)
        return lax.top_k(stays * span + shuffled, K)[1].astype(jnp.int32)
    return jax.vmap(cluster_seeds)(jnp.arange(COARSE, dtype=jnp.int32))


def draw_embeddings(key, part):
    key_one = jax.random.fold_in(jax.random.fold_in(key, 3), 0)
    key_blank = jax.random.fold_in(key, 7)
    values = jax.random.normal(key_one, (TOTAL, D), jnp.float32)
    labels = route_plan(key)[0]
    home = jnp.arange(TOTAL, dtype=jnp.int32) // (ROWS * MEMBERS)
    moving = labels != home
    lottery = jax.random.randint(key_blank, (TOTAL,), 0, 24)
    row_in_device = jnp.arange(TOTAL, dtype=jnp.int32) % ROWS
    first_device = jnp.arange(TOTAL, dtype=jnp.int32) < ROWS
    first_staying = first_device & jnp.logical_not(moving) & (jnp.cumsum((jnp.logical_not(moving) & first_device).astype(jnp.int32)) == 1)
    blank = moving & (lottery == 0) | first_staying | moving & (row_in_device == 0)
    values = jnp.where(blank[:, None], 0.0, values)
    return jnp.clip(values, -20.0, 20.0).astype(jnp.bfloat16)


def draw_kappa(key, part):
    uniform_draw = jax.random.uniform(jax.random.fold_in(key, 5), (COARSE,), jnp.float32)
    lowest = 8.0
    highest = 64.0
    return jnp.exp(jnp.log(lowest) + uniform_draw * (jnp.log(highest) - jnp.log(lowest)))


def setup_inputs(seed: int = 0) -> dict:
    seeds = jax.random.split(jax.random.key(seed), 6)
    return {
        "embeddings": draw_embeddings(jax.random.fold_in(seeds[5], 71), 0),
        "new_label": draw_new_label(jax.random.fold_in(seeds[5], 71), 0),
        "dest_member": draw_dest_member(jax.random.fold_in(seeds[5], 71), 0),
        "seed_index": draw_seed_index(jax.random.fold_in(seeds[5], 71), 0),
        "kappa": draw_kappa(jax.random.fold_in(seeds[5], 71), 0),
    }


EPSILON = 1e-06

def unit_rows(embedded):
    values = embedded.astype(jnp.float32)
    scale = lax.rsqrt(lax.optimization_barrier(jnp.sum(values * values, axis=-1, keepdims=True)) + EPSILON)
    return (values * scale).astype(jnp.bfloat16)

def expectation(normed, alive, centres, concentration):
    scores = concentration * jnp.dot(normed, centres.T, preferred_element_type=jnp.float32)
    largest = lax.optimization_barrier(jnp.max(scores, axis=-1, keepdims=True))
    powered = jnp.exp(scores - largest)
    summed = lax.optimization_barrier(jnp.sum(powered, axis=-1, keepdims=True))
    weights = (powered / summed * alive[:, None]).astype(jnp.bfloat16)
    log_norm = (largest[:, 0] + jnp.log(summed[:, 0])) * alive
    return (weights, log_norm)

def normalise(summed):
    length = jnp.sqrt(lax.optimization_barrier(jnp.sum(summed * summed, axis=-1, keepdims=True)))
    return (summed / jnp.maximum(length, 1.0)).astype(jnp.bfloat16)

def slot_sources(new_label, dest_member):
    devices = COARSE * MEMBERS
    labels = new_label.reshape(devices, ROWS)
    targets = dest_member.reshape(devices, ROWS)
    anchors = jnp.arange(devices, dtype=jnp.int32)
    positions = jnp.arange(ROWS, dtype=jnp.int32)

    def device_spots(packed):
        label_row, target_row, anchor = packed
        moving = label_row != anchor // MEMBERS
        target = label_row * MEMBERS + target_row
        matches = (target[:, None] == target[None, :]) & (positions[None, :] < positions[:, None]) & moving[None, :]
        earlier = lax.optimization_barrier(jnp.sum(matches, axis=1)).astype(jnp.int32)
        moved_spot = target * SLOTS + ROWS + anchor * CAP + earlier
        kept_spot = anchor * SLOTS + positions
        return jnp.where(moving, moved_spot, kept_spot).astype(jnp.int32)
    spots = lax.map(device_spots, (labels, targets, anchors)).reshape(-1)
    empty = jnp.full((devices * SLOTS,), TOTAL, jnp.int32)
    return empty.at[spots].set(jnp.arange(TOTAL, dtype=jnp.int32))

def reference(embeddings, new_label, dest_member, seed_index, kappa):
    sources = slot_sources(new_label, dest_member)
    span = MEMBERS * SLOTS

    def cluster_pass(cluster):
        picked = lax.dynamic_slice_in_dim(sources, cluster * span, span)
        alive = (picked < TOTAL).astype(jnp.float32)
        gathered = jnp.take(embeddings, jnp.minimum(picked, TOTAL - 1), axis=0)
        normed = jnp.where(alive[:, None] > 0, unit_rows(gathered), jnp.zeros((), jnp.bfloat16))
        seed_rows = lax.dynamic_index_in_dim(seed_index, cluster, 0, keepdims=False)
        centres = unit_rows(jnp.take(embeddings, cluster * (MEMBERS * ROWS) + seed_rows, axis=0))
        concentration = lax.dynamic_index_in_dim(kappa, cluster, 0, keepdims=False)
        member_rows = normed.reshape(MEMBERS, SLOTS, D).astype(jnp.float32)
        log_norm = alive
        for iteration in range(ITERS):
            weights, log_norm = expectation(normed, alive, centres, concentration)
            member_weights = weights.reshape(MEMBERS, SLOTS, -1).astype(jnp.float32)
            partial_value = jnp.einsum('msk,msd->mkd', member_weights, member_rows, precision=lax.Precision.HIGHEST)
            partial_value = lax.optimization_barrier(partial_value.astype(jnp.bfloat16)).astype(jnp.float32)
            centres = normalise(lax.optimization_barrier(jnp.sum(partial_value, axis=0)))
        return (centres, log_norm)
    centres, scores = lax.map(cluster_pass, jnp.arange(COARSE, dtype=jnp.int32))
    return (centres.reshape(COARSE * K, D), scores.reshape(-1))
```

```python
import functools

import jax
import jax.numpy as jnp
from jax import lax
from jax.experimental import pallas as pl
from jax.experimental.pallas import tpu as pltpu
from jax.sharding import PartitionSpec as P

ITERS = 2
EPSILON = 1e-06
MESH = pl.DeviceIdType.MESH
F32 = jnp.float32
BF16 = jnp.bfloat16
I32 = jnp.int32


def iota(shape, dim):
    return lax.broadcasted_iota(I32, shape, dim)


def onehot(cond):
    return jnp.where(cond, 1.0, 0.0).astype(BF16)


def nn(a, b):
    return lax.dot_general(a, b, (((1,), (0,)), ((), ())), preferred_element_type=F32)


def nt(a, b):
    return lax.dot_general(a, b, (((1,), (1,)), ((), ())), preferred_element_type=F32)


def tn(a, b):
    return lax.dot_general(a, b, (((0,), (0,)), ((), ())), preferred_element_type=F32)


def rows_at(index, size):
    return pl.ds(pl.multiple_of(index * size, size), size)


def split3(v):
    hi = v.astype(BF16)
    rest = v - hi.astype(F32)
    mid = rest.astype(BF16)
    low = (rest - mid.astype(F32)).astype(BF16)
    pad = jnp.zeros((13,) + v.shape[1:], F32)
    return jnp.concatenate([hi.astype(F32), mid.astype(F32), low.astype(F32), pad], axis=0).astype(BF16)


def kernel(
    dims,
    x_ref, label_ref, member_ref, seed_ref, kappa_ref,
    cent_ref, score_ref,
    rows, hot, send_a, send_b, mid_a, mid_b, fwd_a, fwd_b,
    weights, part, gather_in, block_out, centres, alive, norms,
    mark_s, mark_1, mark_2, mark_3, flat,
    send_sem, recv_sem,
):
    C, G, R, D, K = dims
    Z = C // 2
    S = Z * G
    kb = K // G
    c = lax.axis_index("clusters")
    g = lax.axis_index("group")
    z = c // 2
    core = lax.rem(c, 2)

    barrier = pltpu.get_barrier_semaphore()
    for i in range(1, C):
        pl.semaphore_signal(barrier, inc=1, device_id=(lax.rem(c + i, C), g), device_id_type=MESH)
    for i in range(1, G):
        pl.semaphore_signal(barrier, inc=1, device_id=(c, lax.rem(g + i, G)), device_id_type=MESH)

    def send(phase, src, dst, device):
        pltpu.make_async_remote_copy(
            src_ref=src, dst_ref=dst, send_sem=send_sem.at[phase], recv_sem=recv_sem.at[phase],
            device_id=device, device_id_type=MESH,
        ).start()

    def wait_recv(phase, ref):
        pltpu.make_async_copy(ref, ref, recv_sem.at[phase]).wait()

    def wait_send(phase, ref):
        pltpu.make_async_copy(ref, ref, send_sem.at[phase]).wait()

    ncol = min(D, 256)

    def product(dst, dst_rows, lhs, rhs_ref, rhs_rows):
        @pl.loop(0, D // ncol)
        def _(j):
            cols = rows_at(j, ncol)
            dst[dst_rows, cols] = nn(lhs, rhs_ref[rhs_rows, cols]).astype(BF16)

    rstep = min(R, 128)

    @pl.loop(0, R // rstep)
    def _(i):
        at = rows_at(i, rstep)
        v = x_ref[at, :].astype(F32)
        scale = lax.rsqrt(jnp.sum(v * v, axis=-1, keepdims=True) + EPSILON)
        rows[at, :] = (v * scale).astype(BF16)

    label = label_ref[...]
    member = member_ref[...]
    moving = label != c
    lz = lax.shift_right_logical(label, 1)
    same = (label & 1) == core
    to_a = jnp.where(moving & same, lz * G + member, -1)
    to_b = jnp.where(moving & jnp.logical_not(same), member * Z + lz, -1)
    own = pl.ds(0, R)

    hot[0:S, 0:R] = onehot(iota((S, R), 0) == to_a)
    product(send_a, slice(None), hot[0:S, 0:R], rows, own)
    pl.semaphore_wait(barrier, C - 1 + G - 1)
    for i in range(1, Z):
        tz = lax.rem(z + i, Z)
        send(0, send_a.at[rows_at(tz, G)], mid_a.at[rows_at(z, G)], (tz * 2 + core, g))
    hot[0:S, 0:R] = onehot(iota((S, R), 0) == to_b)
    product(send_b, slice(None), hot[0:S, 0:R], rows, own)
    for i in range(1, G):
        tg = lax.rem(g + i, G)
        send(1, send_b.at[rows_at(tg, Z)], mid_b.at[rows_at(g, Z)], (c, tg))
    mid_a[rows_at(z, G), :] = send_a[rows_at(z, G), :]
    mid_b[rows_at(g, Z), :] = send_b[rows_at(g, Z), :]

    to_cluster = onehot((iota((128, R), 0) == label) & moving)
    to_member = onehot(iota((128, R), 0) == member)
    marks = nt(to_cluster, to_member)
    for i in range(C):
        mark_s[i] = marks[i:i + 1, :]
    for i in range(1, C):
        tc = lax.rem(c + i, C)
        send(2, mark_s.at[tc], mark_1.at[c], (tc, g))
    mark_1[c] = mark_s[c]

    hot[0:R, 0:K] = onehot(iota((R, K), 0) + g * R == seed_ref[...])

    @pl.loop(0, D // ncol)
    def _(j):
        cols = rows_at(j, ncol)
        part[:, cols] = tn(hot[0:R, 0:K], rows[own, cols]).astype(BF16)

    def scatter(phase, first, last):
        for b in range(first, last):
            @pl.when(b != g)
            def _():
                send(phase, part.at[pl.ds(b * kb, kb)], gather_in.at[g], (c, b))

    def gathered_sum(phase):
        wait_recv(phase, gather_in.at[pl.ds(0, G - 1)])
        gather_in[g] = part[rows_at(g, kb), :]
        return jnp.sum(gather_in[...].astype(F32), axis=0)

    def spread(phase, block):
        block_out[...] = block
        for i in range(1, G):
            send(phase, block_out, centres.at[rows_at(g, kb)], (c, lax.rem(g + i, G)))
        centres[rows_at(g, kb), :] = block

    def spread_wait(phase):
        wait_recv(phase, centres.at[pl.ds(0, (G - 1) * kb)])

    scatter(3, 0, G)

    turn_b = onehot((iota((S, S), 0) & (G - 1)) * Z + lax.div(iota((S, S), 0), G) == iota((S, S), 1))
    wait_recv(1, mid_b.at[pl.ds(0, S - Z)])
    product(fwd_b, slice(None), turn_b, mid_b, slice(None))
    base_b = R + S
    for i in range(Z):
        tz = lax.rem(z + i, Z)
        send(5, fwd_b.at[rows_at(tz, G)], rows.at[pl.ds(pl.multiple_of(base_b + z * G, G), G)], (tz * 2 + 1 - core, g))

    wait_recv(2, mark_s.at[pl.ds(0, C - 1)])
    flat[...] = jnp.zeros_like(flat)
    for i in range(C):
        flat[i:i + 1, :] = mark_1[i]
    eye = onehot(iota((16, 128), 0) == iota((16, 128), 1))
    turned = nt(eye, flat[...].astype(BF16))
    for i in range(G):
        mark_2[i] = turned[i:i + 1, :]
    for i in range(1, G):
        tg = lax.rem(g + i, G)
        send(6, mark_2.at[tg], mark_3.at[g], (c, tg))
    mark_3[g] = mark_2[g]

    first_block = gathered_sum(3)
    spread(7, first_block.astype(BF16))

    turn_a = onehot((iota((S, S), 0) & (Z - 1)) * G + lax.div(iota((S, S), 0), Z) == iota((S, S), 1))
    wait_recv(0, mid_a.at[pl.ds(0, S - G)])
    product(fwd_a, slice(None), turn_a, mid_a, slice(None))
    for i in range(1, G):
        tg = lax.rem(g + i, G)
        send(8, fwd_a.at[rows_at(tg, Z)], rows.at[pl.ds(pl.multiple_of(R + g * Z, Z), Z)], (c, tg))
    rows[pl.ds(pl.multiple_of(R + g * Z, Z), Z), :] = fwd_a[rows_at(g, Z), :]

    wait_recv(6, mark_3.at[pl.ds(0, G - 1)])
    for i in range(G):
        flat[i:i + 1, :] = mark_3[i]
    held = flat[0:16, :].astype(BF16)
    alive[:, 0:R] = jnp.where(moving, 0.0, 1.0)
    lane = iota((128, S), 1)
    src = iota((128, S), 0)
    at_a = nn(held, onehot(src == 2 * (lane & (Z - 1)) + core))
    at_b = nn(held, onehot(src == 2 * lax.div(lane, G) + 1 - core))
    lane = iota((16, S), 1)
    src = iota((16, S), 0)
    alive[:, R:R + S] = jnp.sum(jnp.where(lax.div(lane, Z) == src, at_a, 0.0), axis=0, keepdims=True)
    alive[:, R + S:] = jnp.sum(jnp.where((lane & (G - 1)) == src, at_b, 0.0), axis=0, keepdims=True)

    kappa = kappa_ref[0]
    step = S

    def expectation(i):
        at = rows_at(i, step)
        scores = kappa * nt(centres[...], rows[at, :])
        largest = jnp.max(scores, axis=0, keepdims=True)
        powered = jnp.exp(scores - largest)
        summed = jnp.sum(powered, axis=0, keepdims=True)
        here = alive[:, at]
        weights[:, at] = (powered * (1.0 / summed) * here).astype(BF16)
        norms[:, at] = (largest + jnp.log(summed)) * here

    own_steps = R // step
    spread_wait(7)
    pl.loop(0, own_steps)(expectation)
    wait_recv(8, rows.at[pl.ds(0, S - Z)])
    expectation(own_steps)
    wait_recv(5, rows.at[pl.ds(0, S)])
    expectation(own_steps + 1)
    wait_send(3, part.at[pl.ds(0, (G - 1) * kb)])

    half = K // 2
    for it in range(ITERS):
        if it:
            pl.loop(0, own_steps + 2)(expectation)
        for m in range(2):
            product(part, slice(m * half, (m + 1) * half), weights[m * half:(m + 1) * half, :], rows, slice(None))
            scatter(9 + 2 * it, m * G // 2, (m + 1) * G // 2)
        total = gathered_sum(9 + 2 * it)
        length = jnp.sqrt(jnp.sum(total * total, axis=-1, keepdims=True))
        block = (total / jnp.maximum(length, 1.0)).astype(BF16)
        wait_send(7 if it == 0 else 8 + 2 * it, centres.at[pl.ds(0, (G - 1) * kb)])
        spread(10 + 2 * it, block)
        if it == ITERS - 1:
            score_ref[:, 0:R] = norms[:, 0:R]
            lane = iota((S, 2 * S), 1)
            src = iota((S, 2 * S), 0)
            turn = onehot(lane == (src & (Z - 1)) * 2 * G + core * G + lax.div(src, Z))
            moved = nn(split3(norms[:, R:R + S]), turn)
            turn = onehot(lane == lax.div(src, G) * 2 * G + (1 - core) * G + (src & (G - 1)))
            moved = moved + nn(split3(norms[:, R + S:]), turn)
            score_ref[:, R:] = moved[0:1, :] + moved[1:2, :] + moved[2:3, :]
        spread_wait(10 + 2 * it)
        wait_send(9 + 2 * it, part.at[pl.ds(0, (G - 1) * kb)])
    wait_send(10 + 2 * (ITERS - 1), centres.at[pl.ds(0, (G - 1) * kb)])
    cent_ref[...] = centres[...]

    wait_send(0, send_a.at[pl.ds(0, S - G)])
    wait_send(1, send_b.at[pl.ds(0, S - Z)])
    wait_send(2, mark_s.at[pl.ds(0, C - 1)])
    wait_send(5, rows.at[pl.ds(0, S)])
    wait_send(6, mark_3.at[pl.ds(0, G - 1)])
    wait_send(8, rows.at[pl.ds(0, S - Z)])


def shards(embeddings, new_label, dest_member, seed_index, kappa):
    R, D = embeddings.shape
    K = seed_index.shape[1]
    C = lax.axis_size("clusters")
    G = lax.axis_size("group")
    S = C * G // 2
    kb = K // G
    slots = R + 2 * S
    vmem = pl.BlockSpec(memory_space=pltpu.VMEM)
    phases = 10 + 2 * ITERS
    centroids, score = pl.pallas_call(
        functools.partial(kernel, (C, G, R, D, K)),
        name="refine",
        out_shape=(
            jax.ShapeDtypeStruct((K, D), BF16),
            jax.ShapeDtypeStruct((1, slots), F32),
        ),
        in_specs=[vmem, vmem, vmem, vmem, pl.BlockSpec(memory_space=pltpu.SMEM)],
        out_specs=(vmem, vmem),
        scratch_shapes=[
            pltpu.VMEM((slots, D), BF16),
            pltpu.VMEM((max(R, K), max(R, K)), BF16),
            pltpu.VMEM((S, D), BF16),
            pltpu.VMEM((S, D), BF16),
            pltpu.VMEM((S, D), BF16),
            pltpu.VMEM((S, D), BF16),
            pltpu.VMEM((S, D), BF16),
            pltpu.VMEM((S, D), BF16),
            pltpu.VMEM((K, slots), BF16),
            pltpu.VMEM((K, D), BF16),
            pltpu.VMEM((G, kb, D), BF16),
            pltpu.VMEM((kb, D), BF16),
            pltpu.VMEM((K, D), BF16),
            pltpu.VMEM((1, slots), F32),
            pltpu.VMEM((1, slots), F32),
            pltpu.VMEM((C, 1, 128), F32),
            pltpu.VMEM((C, 1, 128), F32),
            pltpu.VMEM((G, 1, 128), F32),
            pltpu.VMEM((G, 1, 128), F32),
            pltpu.VMEM((128, 128), F32),
            pltpu.SemaphoreType.DMA((phases,)),
            pltpu.SemaphoreType.DMA((phases,)),
        ],
        compiler_params=pltpu.CompilerParams(
            collective_id=0, has_side_effects=True, vmem_limit_bytes=40 * 1024 * 1024
        ),
    )(
        embeddings,
        new_label.reshape(1, R),
        dest_member.reshape(1, R),
        seed_index,
        kappa,
    )
    return centroids, score.reshape(slots)


def solution(mesh):
    return jax.shard_map(
        shards,
        mesh=mesh,
        in_specs=(
            P(("clusters", "group"), None),
            P(("clusters", "group")),
            P(("clusters", "group")),
            P("clusters", None),
            P("clusters"),
        ),
        out_specs=(P("clusters", None), P(("clusters", "group"))),
        check_vma=False,
    )
```

```python
import functools

import jax
import jax.numpy as jnp
from jax import lax
from jax.experimental import pallas as pl
from jax.experimental.pallas import tpu as pltpu
from jax.sharding import PartitionSpec as P

ITERS = 2
EPSILON = 1e-06
MESH = pl.DeviceIdType.MESH
F32 = jnp.float32
BF16 = jnp.bfloat16
I32 = jnp.int32


def iota(shape, dim):
    return lax.broadcasted_iota(I32, shape, dim)


def onehot(cond):
    return jnp.where(cond, 1.0, 0.0).astype(BF16)


def nn(a, b):
    return lax.dot_general(a, b, (((1,), (0,)), ((), ())), preferred_element_type=F32)


def nt(a, b):
    return lax.dot_general(a, b, (((1,), (1,)), ((), ())), preferred_element_type=F32)


def tn(a, b):
    return lax.dot_general(a, b, (((0,), (0,)), ((), ())), preferred_element_type=F32)


def rows_at(index, size):
    return pl.ds(pl.multiple_of(index * size, size), size)


def split3(v):
    hi = v.astype(BF16)
    rest = v - hi.astype(F32)
    mid = rest.astype(BF16)
    low = (rest - mid.astype(F32)).astype(BF16)
    pad = jnp.zeros((13,) + v.shape[1:], F32)
    return jnp.concatenate([hi.astype(F32), mid.astype(F32), low.astype(F32), pad], axis=0).astype(BF16)


def kernel(
    dims,
    x_hbm, label_hbm, member_hbm, seed_hbm, kappa_ref,
    cent_hbm, score_hbm,
    x_ref, label_ref, member_ref, seed_ref, score_ref,
    rows, hot, send_a, send_b, mid_a, mid_b, fwd_a, fwd_b,
    weights, part, gather_in, block_out, centres, alive, norms,
    mark_s, mark_1, mark_2, mark_3, flat,
    send_sem, recv_sem, load_sem,
):
    C, G, R, D, K = dims
    Z = C // 2
    S = Z * G
    kb = K // G
    c = lax.axis_index("clusters")
    g = lax.axis_index("group")
    z = c // 2
    core = lax.rem(c, 2)

    barrier = pltpu.get_barrier_semaphore()
    for i in range(1, C):
        pl.semaphore_signal(barrier, inc=1, device_id=(lax.rem(c + i, C), g), device_id_type=MESH)
    for i in range(1, G):
        pl.semaphore_signal(barrier, inc=1, device_id=(c, lax.rem(g + i, G)), device_id_type=MESH)

    loads = [
        pltpu.make_async_copy(src, dst, load_sem.at[i])
        for i, (src, dst) in enumerate(
            ((label_hbm, label_ref), (member_hbm, member_ref), (x_hbm, x_ref), (seed_hbm, seed_ref))
        )
    ]
    for load in loads:
        load.start()

    def send(phase, src, dst, device):
        pltpu.make_async_remote_copy(
            src_ref=src, dst_ref=dst, send_sem=send_sem.at[phase], recv_sem=recv_sem.at[phase],
            device_id=device, device_id_type=MESH,
        ).start()

    def wait_recv(phase, ref):
        pltpu.make_async_copy(ref, ref, recv_sem.at[phase]).wait()

    def wait_send(phase, ref):
        pltpu.make_async_copy(ref, ref, send_sem.at[phase]).wait()

    ncol = min(D, 256)

    def product(dst, dst_rows, lhs, rhs_ref, rhs_rows):
        @pl.loop(0, D // ncol)
        def _(j):
            cols = rows_at(j, ncol)
            dst[dst_rows, cols] = nn(lhs, rhs_ref[rhs_rows, cols]).astype(BF16)

    loads[2].wait()
    rstep = min(R, 128)

    @pl.loop(0, R // rstep)
    def _(i):
        at = rows_at(i, rstep)
        v = x_ref[at, :].astype(F32)
        scale = lax.rsqrt(jnp.sum(v * v, axis=-1, keepdims=True) + EPSILON)
        rows[at, :] = (v * scale).astype(BF16)

    loads[0].wait()
    loads[1].wait()
    loads[3].wait()
    label = label_ref[...]
    member = member_ref[...]
    moving = label != c
    lz = lax.shift_right_logical(label, 1)
    same = (label & 1) == core
    to_a = jnp.where(moving & same, lz * G + member, -1)
    to_b = jnp.where(moving & jnp.logical_not(same), member * Z + lz, -1)
    own = pl.ds(0, R)

    to_cluster = onehot((iota((128, R), 0) == label) & moving)
    to_member = onehot(iota((128, R), 0) == member)
    marks = nt(to_cluster, to_member)
    for i in range(C):
        mark_s[i] = marks[i:i + 1, :]
    mark_1[c] = mark_s[c]
    hot[0:S, 0:R] = onehot(iota((S, R), 0) == to_a)
    product(send_a, slice(None), hot[0:S, 0:R], rows, own)
    hot[0:S, 0:R] = onehot(iota((S, R), 0) == to_b)
    product(send_b, slice(None), hot[0:S, 0:R], rows, own)

    pl.semaphore_wait(barrier, C - 1 + G - 1)
    for i in range(1, C):
        tc = lax.rem(c + i, C)
        send(2, mark_s.at[tc], mark_1.at[c], (tc, g))
    for i in range(1, G):
        tg = lax.rem(g + i, G)
        send(1, send_b.at[rows_at(tg, Z)], mid_b.at[rows_at(g, Z)], (c, tg))
    for i in range(1, Z):
        tz = lax.rem(z + i, Z)
        send(0, send_a.at[rows_at(tz, G)], mid_a.at[rows_at(z, G)], (tz * 2 + core, g))
    mid_a[rows_at(z, G), :] = send_a[rows_at(z, G), :]
    mid_b[rows_at(g, Z), :] = send_b[rows_at(g, Z), :]

    hot[0:R, 0:K] = onehot(iota((R, K), 0) + g * R == seed_ref[...])

    @pl.loop(0, D // ncol)
    def _(j):
        cols = rows_at(j, ncol)
        part[:, cols] = tn(hot[0:R, 0:K], rows[own, cols]).astype(BF16)

    def scatter(phase, first, last):
        for b in range(first, last):
            @pl.when(b != g)
            def _():
                send(phase, part.at[pl.ds(b * kb, kb)], gather_in.at[g], (c, b))

    def gathered_sum(phase):
        wait_recv(phase, gather_in.at[pl.ds(0, G - 1)])
        gather_in[g] = part[rows_at(g, kb), :]
        return jnp.sum(gather_in[...].astype(F32), axis=0)

    def spread(phase, block):
        block_out[...] = block
        for i in range(1, G):
            send(phase, block_out, centres.at[rows_at(g, kb)], (c, lax.rem(g + i, G)))
        centres[rows_at(g, kb), :] = block

    def spread_wait(phase):
        wait_recv(phase, centres.at[pl.ds(0, (G - 1) * kb)])

    turn_b = onehot((iota((S, S), 0) & (G - 1)) * Z + lax.div(iota((S, S), 0), G) == iota((S, S), 1))
    wait_recv(1, mid_b.at[pl.ds(0, S - Z)])
    scatter(3, 0, G)
    product(fwd_b, slice(None), turn_b, mid_b, slice(None))
    base_b = R + S
    for i in range(Z):
        tz = lax.rem(z + i, Z)
        send(5, fwd_b.at[rows_at(tz, G)], rows.at[pl.ds(pl.multiple_of(base_b + z * G, G), G)], (tz * 2 + 1 - core, g))

    wait_recv(2, mark_s.at[pl.ds(0, C - 1)])
    flat[...] = jnp.zeros_like(flat)
    for i in range(C):
        flat[i:i + 1, :] = mark_1[i]
    eye = onehot(iota((16, 128), 0) == iota((16, 128), 1))
    turned = nt(eye, flat[...].astype(BF16))
    for i in range(G):
        mark_2[i] = turned[i:i + 1, :]
    for i in range(1, G):
        tg = lax.rem(g + i, G)
        send(6, mark_2.at[tg], mark_3.at[g], (c, tg))
    mark_3[g] = mark_2[g]

    first_block = gathered_sum(3)
    spread(7, first_block.astype(BF16))

    turn_a = onehot((iota((S, S), 0) & (Z - 1)) * G + lax.div(iota((S, S), 0), Z) == iota((S, S), 1))
    wait_recv(0, mid_a.at[pl.ds(0, S - G)])
    product(fwd_a, slice(None), turn_a, mid_a, slice(None))
    for i in range(1, G):
        tg = lax.rem(g + i, G)
        send(8, fwd_a.at[rows_at(tg, Z)], rows.at[pl.ds(pl.multiple_of(R + g * Z, Z), Z)], (c, tg))
    rows[pl.ds(pl.multiple_of(R + g * Z, Z), Z), :] = fwd_a[rows_at(g, Z), :]

    wait_recv(6, mark_3.at[pl.ds(0, G - 1)])
    for i in range(G):
        flat[i:i + 1, :] = mark_3[i]
    held = flat[0:16, :].astype(BF16)
    alive[:, 0:R] = jnp.where(moving, 0.0, 1.0)
    lane = iota((128, S), 1)
    src = iota((128, S), 0)
    at_a = nn(held, onehot(src == 2 * (lane & (Z - 1)) + core))
    at_b = nn(held, onehot(src == 2 * lax.div(lane, G) + 1 - core))
    lane = iota((16, S), 1)
    src = iota((16, S), 0)
    alive[:, R:R + S] = jnp.sum(jnp.where(lax.div(lane, Z) == src, at_a, 0.0), axis=0, keepdims=True)
    alive[:, R + S:] = jnp.sum(jnp.where((lane & (G - 1)) == src, at_b, 0.0), axis=0, keepdims=True)

    kappa = kappa_ref[0]
    step = S

    def expectation(i):
        at = rows_at(i, step)
        scores = kappa * nt(centres[...], rows[at, :])
        largest = jnp.max(scores, axis=0, keepdims=True)
        powered = jnp.exp(scores - largest)
        summed = jnp.sum(powered, axis=0, keepdims=True)
        here = alive[:, at]
        weights[:, at] = (powered * (1.0 / summed) * here).astype(BF16)
        norms[:, at] = (largest + jnp.log(summed)) * here

    own_steps = R // step
    spread_wait(7)
    pl.loop(0, own_steps)(expectation)
    wait_recv(8, rows.at[pl.ds(0, S - Z)])
    expectation(own_steps)
    wait_recv(5, rows.at[pl.ds(0, S)])
    expectation(own_steps + 1)
    wait_send(3, part.at[pl.ds(0, (G - 1) * kb)])

    half = K // 2
    put_scores = pltpu.make_async_copy(score_ref, score_hbm, load_sem.at[0])
    put_centres = pltpu.make_async_copy(centres, cent_hbm, load_sem.at[1])
    for it in range(ITERS):
        if it:
            pl.loop(0, own_steps + 2)(expectation)
        for m in range(2):
            product(part, slice(m * half, (m + 1) * half), weights[m * half:(m + 1) * half, :], rows, slice(None))
            scatter(9 + 2 * it, m * G // 2, (m + 1) * G // 2)
        total = gathered_sum(9 + 2 * it)
        length = jnp.sqrt(jnp.sum(total * total, axis=-1, keepdims=True))
        block = (total / jnp.maximum(length, 1.0)).astype(BF16)
        wait_send(7 if it == 0 else 8 + 2 * it, centres.at[pl.ds(0, (G - 1) * kb)])
        spread(10 + 2 * it, block)
        if it == ITERS - 1:
            score_ref[:, 0:R] = norms[:, 0:R]
            lane = iota((S, 2 * S), 1)
            src = iota((S, 2 * S), 0)
            turn = onehot(lane == (src & (Z - 1)) * 2 * G + core * G + lax.div(src, Z))
            moved = nn(split3(norms[:, R:R + S]), turn)
            turn = onehot(lane == lax.div(src, G) * 2 * G + (1 - core) * G + (src & (G - 1)))
            moved = moved + nn(split3(norms[:, R + S:]), turn)
            score_ref[:, R:] = moved[0:1, :] + moved[1:2, :] + moved[2:3, :]
            put_scores.start()
        spread_wait(10 + 2 * it)
        wait_send(9 + 2 * it, part.at[pl.ds(0, (G - 1) * kb)])
    wait_send(10 + 2 * (ITERS - 1), centres.at[pl.ds(0, (G - 1) * kb)])
    put_centres.start()
    put_centres.wait()
    put_scores.wait()

    wait_send(0, send_a.at[pl.ds(0, S - G)])
    wait_send(1, send_b.at[pl.ds(0, S - Z)])
    wait_send(2, mark_s.at[pl.ds(0, C - 1)])
    wait_send(5, rows.at[pl.ds(0, S)])
    wait_send(6, mark_3.at[pl.ds(0, G - 1)])
    wait_send(8, rows.at[pl.ds(0, S - Z)])


def shards(embeddings, new_label, dest_member, seed_index, kappa):
    R, D = embeddings.shape
    K = seed_index.shape[1]
    C = lax.axis_size("clusters")
    G = lax.axis_size("group")
    S = C * G // 2
    kb = K // G
    slots = R + 2 * S
    hbm = pl.BlockSpec(memory_space=pltpu.HBM)
    phases = 10 + 2 * ITERS
    centroids, score = pl.pallas_call(
        functools.partial(kernel, (C, G, R, D, K)),
        name="refine",
        out_shape=(
            jax.ShapeDtypeStruct((K, D), BF16),
            jax.ShapeDtypeStruct((1, slots), F32),
        ),
        in_specs=[hbm, hbm, hbm, hbm, pl.BlockSpec(memory_space=pltpu.SMEM)],
        out_specs=(hbm, hbm),
        scratch_shapes=[
            pltpu.VMEM((R, D), BF16),
            pltpu.VMEM((1, R), I32),
            pltpu.VMEM((1, R), I32),
            pltpu.VMEM((1, K), I32),
            pltpu.VMEM((1, slots), F32),
            pltpu.VMEM((slots, D), BF16),
            pltpu.VMEM((max(R, K), max(R, K)), BF16),
            pltpu.VMEM((S, D), BF16),
            pltpu.VMEM((S, D), BF16),
            pltpu.VMEM((S, D), BF16),
            pltpu.VMEM((S, D), BF16),
            pltpu.VMEM((S, D), BF16),
            pltpu.VMEM((S, D), BF16),
            pltpu.VMEM((K, slots), BF16),
            pltpu.VMEM((K, D), BF16),
            pltpu.VMEM((G, kb, D), BF16),
            pltpu.VMEM((kb, D), BF16),
            pltpu.VMEM((K, D), BF16),
            pltpu.VMEM((1, slots), F32),
            pltpu.VMEM((1, slots), F32),
            pltpu.VMEM((C, 1, 128), F32),
            pltpu.VMEM((C, 1, 128), F32),
            pltpu.VMEM((G, 1, 128), F32),
            pltpu.VMEM((G, 1, 128), F32),
            pltpu.VMEM((128, 128), F32),
            pltpu.SemaphoreType.DMA((phases,)),
            pltpu.SemaphoreType.DMA((phases,)),
            pltpu.SemaphoreType.DMA((4,)),
        ],
        compiler_params=pltpu.CompilerParams(
            collective_id=0, has_side_effects=True, vmem_limit_bytes=60 * 1024 * 1024
        ),
    )(
        embeddings,
        new_label.reshape(1, R),
        dest_member.reshape(1, R),
        seed_index,
        kappa,
    )
    return centroids, score.reshape(slots)


def solution(mesh):
    return jax.shard_map(
        shards,
        mesh=mesh,
        in_specs=(
            P(("clusters", "group"), None),
            P(("clusters", "group")),
            P(("clusters", "group")),
            P("clusters", None),
            P("clusters"),
        ),
        out_specs=(P("clusters", None), P(("clusters", "group"))),
        check_vma=False,
    )
```

```python
import functools

import jax
import jax.numpy as jnp
from jax import lax
from jax.experimental import pallas as pl
from jax.experimental.pallas import tpu as pltpu
from jax.sharding import PartitionSpec as P

ITERS = 2
EPSILON = 1e-06
MESH = pl.DeviceIdType.MESH
F32 = jnp.float32
BF16 = jnp.bfloat16
I32 = jnp.int32


def iota(shape, dim):
    return lax.broadcasted_iota(I32, shape, dim)


def onehot(cond):
    return jnp.where(cond, 1.0, 0.0).astype(BF16)


def nn(a, b):
    return lax.dot_general(a, b, (((1,), (0,)), ((), ())), preferred_element_type=F32)


def nt(a, b):
    return lax.dot_general(a, b, (((1,), (1,)), ((), ())), preferred_element_type=F32)


def tn(a, b):
    return lax.dot_general(a, b, (((0,), (0,)), ((), ())), preferred_element_type=F32)


def rows_at(index, size):
    return pl.ds(pl.multiple_of(index * size, size), size)


def split3(v):
    hi = v.astype(BF16)
    rest = v - hi.astype(F32)
    mid = rest.astype(BF16)
    low = (rest - mid.astype(F32)).astype(BF16)
    pad = jnp.zeros((13,) + v.shape[1:], F32)
    return jnp.concatenate([hi.astype(F32), mid.astype(F32), low.astype(F32), pad], axis=0).astype(BF16)


def kernel(
    dims,
    x_hbm, label_hbm, member_hbm, seed_hbm, kappa_ref,
    cent_hbm, score_hbm,
    x_ref, label_ref, member_ref, seed_ref, score_ref,
    rows, hot, send_a, send_b, mid_a, mid_b, fwd_a, fwd_b,
    weights, part, relay, combined, nearer, line, line_in, centres, alive, norms,
    mark_s, mark_1, mark_2, mark_3, flat,
    send_sem, recv_sem, load_sem, plane_send, rs_sem, rs_line_sem, ag_sem, ag_line_sem,
):
    C, G, R, D, K = dims
    Z = C // 2
    S = Z * G
    kb = K // G
    c = lax.axis_index("clusters")
    g = lax.axis_index("group")
    z = c // 2
    core = lax.rem(c, 2)

    barrier = pltpu.get_barrier_semaphore()
    for i in range(1, C):
        pl.semaphore_signal(barrier, inc=1, device_id=(lax.rem(c + i, C), g), device_id_type=MESH)
    for i in range(1, G):
        pl.semaphore_signal(barrier, inc=1, device_id=(c, lax.rem(g + i, G)), device_id_type=MESH)

    loads = [
        pltpu.make_async_copy(src, dst, load_sem.at[i])
        for i, (src, dst) in enumerate(
            ((label_hbm, label_ref), (member_hbm, member_ref), (x_hbm, x_ref), (seed_hbm, seed_ref))
        )
    ]
    for load in loads:
        load.start()

    def send(phase, src, dst, device):
        pltpu.make_async_remote_copy(
            src_ref=src, dst_ref=dst, send_sem=send_sem.at[phase], recv_sem=recv_sem.at[phase],
            device_id=device, device_id_type=MESH,
        ).start()

    def wait_recv(phase, ref):
        pltpu.make_async_copy(ref, ref, recv_sem.at[phase]).wait()

    def wait_send(phase, ref):
        pltpu.make_async_copy(ref, ref, send_sem.at[phase]).wait()

    ncol = min(D, 256)

    def product(dst, dst_rows, lhs, rhs_ref, rhs_rows):
        @pl.loop(0, D // ncol)
        def _(j):
            cols = rows_at(j, ncol)
            dst[dst_rows, cols] = nn(lhs, rhs_ref[rhs_rows, cols]).astype(BF16)

    loads[2].wait()
    rstep = min(R, 128)

    @pl.loop(0, R // rstep)
    def _(i):
        at = rows_at(i, rstep)
        v = x_ref[at, :].astype(F32)
        scale = lax.rsqrt(jnp.sum(v * v, axis=-1, keepdims=True) + EPSILON)
        rows[at, :] = (v * scale).astype(BF16)

    loads[0].wait()
    loads[1].wait()
    loads[3].wait()
    label = label_ref[...]
    member = member_ref[...]
    moving = label != c
    lz = lax.shift_right_logical(label, 1)
    same = (label & 1) == core
    to_a = jnp.where(moving & same, lz * G + member, -1)
    to_b = jnp.where(moving & jnp.logical_not(same), member * Z + lz, -1)
    own = pl.ds(0, R)

    to_cluster = onehot((iota((128, R), 0) == label) & moving)
    to_member = onehot(iota((128, R), 0) == member)
    marks = nt(to_cluster, to_member)
    for i in range(C):
        mark_s[i] = marks[i:i + 1, :]
    mark_1[c] = mark_s[c]
    hot[0:S, 0:R] = onehot(iota((S, R), 0) == to_a)
    product(send_a, slice(None), hot[0:S, 0:R], rows, own)
    hot[0:S, 0:R] = onehot(iota((S, R), 0) == to_b)
    product(send_b, slice(None), hot[0:S, 0:R], rows, own)

    pl.semaphore_wait(barrier, C - 1 + G - 1)
    for i in range(1, C):
        tc = lax.rem(c + i, C)
        send(2, mark_s.at[tc], mark_1.at[c], (tc, g))
    for i in range(1, G):
        tg = lax.rem(g + i, G)
        send(1, send_b.at[rows_at(tg, Z)], mid_b.at[rows_at(g, Z)], (c, tg))
    for i in range(1, Z):
        tz = lax.rem(z + i, Z)
        send(0, send_a.at[rows_at(tz, G)], mid_a.at[rows_at(z, G)], (tz * 2 + core, g))
    mid_a[rows_at(z, G), :] = send_a[rows_at(z, G), :]
    mid_b[rows_at(g, Z), :] = send_b[rows_at(g, Z), :]

    n = round(G ** 0.5)
    hb = kb // 2
    Dh = D // 2
    px, py = g // n, lax.rem(g, n)
    first = (px, py)
    second = (py, px)
    ORDER = (2, 1, 3, 0)

    def at_plane(h, p, o):
        p, o = lax.rem(p + n, n), lax.rem(o + n, n)
        return p * n + o if h == 0 else o * n + p

    def block(h, dp, do):
        return at_plane(h, first[h] + dp, second[h] + do)

    def part_of(b, half=None):
        if half is None:
            return pl.ds(pl.multiple_of(b * kb, kb), kb)
        return pl.ds(pl.multiple_of(b * kb + half * hb, hb), hb)

    def push(phase, src, dst, sem, b):
        pltpu.make_async_remote_copy(
            src_ref=src, dst_ref=dst, send_sem=plane_send.at[phase], recv_sem=sem,
            device_id=(c, b), device_id_type=MESH,
        ).start()

    def landed(ref, sem):
        pltpu.make_async_copy(ref, ref, sem).wait()

    def sent(phase):
        for h in range(2):
            ref = part.at[h, pl.ds(0, (G - 1) * kb)]
            pltpu.make_async_copy(ref, ref, plane_send.at[phase]).wait()

    TOP, LOW = pl.ds(0, hb), pl.ds(hb, hb)

    def reduce_scatter(fill):
        for h in range(2):
            fill(h)
            ahead, behind = block(h, 1, 0), block(h, -1, 0)
            for r in ORDER:
                far = block(h, 2, r)
                push(0, part.at[h, part_of(far, 0)], relay.at[h, r, TOP], rs_sem.at[h, r, 0], ahead)
                push(0, part.at[h, part_of(far, 1)], relay.at[h, r, LOW], rs_sem.at[h, r, 1], behind)
            for r in ORDER:
                push(0, part.at[h, part_of(block(h, 1, r), 1)], nearer.at[h, r, 0, LOW], rs_sem.at[h, r, 2], ahead)
                push(0, part.at[h, part_of(block(h, -1, r), 0)], nearer.at[h, r, 1, TOP], rs_sem.at[h, r, 3], behind)
        for r in ORDER:
            for h in range(2):
                ahead, behind = block(h, 1, 0), block(h, -1, 0)
                landed(relay.at[h, r, TOP], rs_sem.at[h, r, 0])
                mine = part[h, part_of(block(h, 1, r), 0), :].astype(F32)
                combined[h, r, TOP, :] = (mine + relay[h, r, TOP, :].astype(F32)).astype(BF16)
                push(0, combined.at[h, r, TOP], nearer.at[h, r, 0, TOP], rs_sem.at[h, r, 4], ahead)
                landed(relay.at[h, r, LOW], rs_sem.at[h, r, 1])
                mine = part[h, part_of(block(h, -1, r), 1), :].astype(F32)
                combined[h, r, LOW, :] = (mine + relay[h, r, LOW, :].astype(F32)).astype(BF16)
                push(0, combined.at[h, r, LOW], nearer.at[h, r, 1, LOW], rs_sem.at[h, r, 5], behind)
        for r in ORDER:
            for h in range(2):
                landed(nearer.at[h, r, 0, LOW], rs_sem.at[h, r, 2])
                landed(nearer.at[h, r, 1, TOP], rs_sem.at[h, r, 3])
                landed(nearer.at[h, r, 0, TOP], rs_sem.at[h, r, 4])
                landed(nearer.at[h, r, 1, LOW], rs_sem.at[h, r, 5])
                total = part[h, part_of(block(h, 0, r)), :].astype(F32)
                total = total + nearer[h, r, 0].astype(F32) + nearer[h, r, 1].astype(F32)
                line[h, r] = total.astype(BF16)
                if r:
                    push(0, line.at[h, r], line_in.at[h, r - 1], rs_line_sem.at[h, r - 1], block(h, 0, r))
        totals = []
        for h in range(2):
            total = line[h, 0].astype(F32)
            for r in range(3):
                landed(line_in.at[h, r], rs_line_sem.at[h, r])
                total = total + line_in[h, r].astype(F32)
            totals.append(total)
        return totals

    def all_gather(blocks, meanwhile=None):
        own_at = part_of(g)
        for h in range(2):
            centres[h, own_at, :] = blocks[h]

        def along(h, r):
            here = part_of(block(h, 0, r))
            push(1, centres.at[h, here], centres.at[h, here], ag_sem.at[h, r, 0], block(h, 1, 0))
            push(1, centres.at[h, here], centres.at[h, here], ag_sem.at[h, r, 1], block(h, -1, 0))
            if r == 2:
                push(1, centres.at[h, here], centres.at[h, here], ag_sem.at[h, r, 2], block(h, 2, 0))

        def forward(h, r):
            back, front = block(h, -1, r), block(h, 1, r)
            landed(centres.at[h, part_of(back)], ag_sem.at[h, r, 0])
            if r != 2:
                top = part_of(back, 0)
                push(1, centres.at[h, top], centres.at[h, top], ag_sem.at[h, r, 2], block(h, 1, 0))
            landed(centres.at[h, part_of(front)], ag_sem.at[h, r, 1])
            if r != 2:
                low = part_of(front, 1)
                push(1, centres.at[h, low], centres.at[h, low], ag_sem.at[h, r, 3], block(h, -1, 0))

        for h in range(2):
            for r in (1, 3, 2):
                push(1, centres.at[h, own_at], centres.at[h, own_at], ag_line_sem.at[h, r - 1], block(h, 0, r))
            along(h, 0)
        if meanwhile is not None:
            meanwhile()
        for r in (3, 1):
            for h in range(2):
                landed(centres.at[h, part_of(block(h, 0, r))], ag_line_sem.at[h, n - r - 1])
                along(h, r)
        for h in range(2):
            forward(h, 0)
        for h in range(2):
            landed(centres.at[h, part_of(block(h, 0, 2))], ag_line_sem.at[h, 1])
            along(h, 2)
        for r in (3, 1, 2):
            for h in range(2):
                forward(h, r)
        for r in (0, 3, 1, 2):
            for h in range(2):
                far = block(h, 2, r)
                if r == 2:
                    landed(centres.at[h, part_of(far)], ag_sem.at[h, r, 2])
                else:
                    landed(centres.at[h, part_of(far, 0)], ag_sem.at[h, r, 2])
                    landed(centres.at[h, part_of(far, 1)], ag_sem.at[h, r, 3])

    hot[0:R, 0:K] = onehot(iota((R, K), 0) + g * R == seed_ref[...])
    hcol = min(Dh, 256)

    def fill_seeds(h):
        @pl.loop(0, Dh // hcol)
        def _(j):
            cols = pl.ds(pl.multiple_of(h * Dh + j * hcol, hcol), hcol)
            part[h, :, rows_at(j, hcol)] = tn(hot[0:R, 0:K], rows[own, cols]).astype(BF16)

    def fill_sums(h):
        @pl.loop(0, Dh // hcol)
        def _(j):
            cols = pl.ds(pl.multiple_of(h * Dh + j * hcol, hcol), hcol)
            part[h, :, rows_at(j, hcol)] = nn(weights[...], rows[:, cols]).astype(BF16)

    turn_b = onehot((iota((S, S), 0) & (G - 1)) * Z + lax.div(iota((S, S), 0), G) == iota((S, S), 1))
    wait_recv(1, mid_b.at[pl.ds(0, S - Z)])
    product(fwd_b, slice(None), turn_b, mid_b, slice(None))
    base_b = R + S
    for i in range(Z):
        tz = lax.rem(z + i, Z)
        send(5, fwd_b.at[rows_at(tz, G)], rows.at[pl.ds(pl.multiple_of(base_b + z * G, G), G)], (tz * 2 + 1 - core, g))

    wait_recv(2, mark_s.at[pl.ds(0, C - 1)])
    flat[...] = jnp.zeros_like(flat)
    for i in range(C):
        flat[i:i + 1, :] = mark_1[i]
    eye = onehot(iota((16, 128), 0) == iota((16, 128), 1))
    turned = nt(eye, flat[...].astype(BF16))
    for i in range(G):
        mark_2[i] = turned[i:i + 1, :]
    for i in range(1, G):
        tg = lax.rem(g + i, G)
        send(6, mark_2.at[tg], mark_3.at[g], (c, tg))
    mark_3[g] = mark_2[g]

    all_gather([t.astype(BF16) for t in reduce_scatter(fill_seeds)])
    sent(0)
    sent(1)

    turn_a = onehot((iota((S, S), 0) & (Z - 1)) * G + lax.div(iota((S, S), 0), Z) == iota((S, S), 1))
    wait_recv(0, mid_a.at[pl.ds(0, S - G)])
    product(fwd_a, slice(None), turn_a, mid_a, slice(None))
    for i in range(1, G):
        tg = lax.rem(g + i, G)
        send(8, fwd_a.at[rows_at(tg, Z)], rows.at[pl.ds(pl.multiple_of(R + g * Z, Z), Z)], (c, tg))
    rows[pl.ds(pl.multiple_of(R + g * Z, Z), Z), :] = fwd_a[rows_at(g, Z), :]

    wait_recv(6, mark_3.at[pl.ds(0, G - 1)])
    for i in range(G):
        flat[i:i + 1, :] = mark_3[i]
    held = flat[0:16, :].astype(BF16)
    alive[:, 0:R] = jnp.where(moving, 0.0, 1.0)
    lane = iota((128, S), 1)
    src = iota((128, S), 0)
    at_a = nn(held, onehot(src == 2 * (lane & (Z - 1)) + core))
    at_b = nn(held, onehot(src == 2 * lax.div(lane, G) + 1 - core))
    lane = iota((16, S), 1)
    src = iota((16, S), 0)
    alive[:, R:R + S] = jnp.sum(jnp.where(lax.div(lane, Z) == src, at_a, 0.0), axis=0, keepdims=True)
    alive[:, R + S:] = jnp.sum(jnp.where((lane & (G - 1)) == src, at_b, 0.0), axis=0, keepdims=True)

    kappa = kappa_ref[0]
    step = S

    def expectation(i):
        at = rows_at(i, step)
        scores = nt(centres[0], rows[at, 0:Dh]) + nt(centres[1], rows[at, Dh:D])
        scores = kappa * scores
        largest = jnp.max(scores, axis=0, keepdims=True)
        powered = jnp.exp(scores - largest)
        summed = jnp.sum(powered, axis=0, keepdims=True)
        here = alive[:, at]
        weights[:, at] = (powered * (1.0 / summed) * here).astype(BF16)
        norms[:, at] = (largest + jnp.log(summed)) * here

    own_steps = R // step
    pl.loop(0, own_steps)(expectation)
    wait_recv(8, rows.at[pl.ds(0, S - Z)])
    expectation(own_steps)
    wait_recv(5, rows.at[pl.ds(0, S)])
    expectation(own_steps + 1)
    put_scores = pltpu.make_async_copy(score_ref, score_hbm, load_sem.at[0])

    def place_scores():
        score_ref[:, 0:R] = norms[:, 0:R]
        lane = iota((S, 2 * S), 1)
        src = iota((S, 2 * S), 0)
        turn = onehot(lane == (src & (Z - 1)) * 2 * G + core * G + lax.div(src, Z))
        moved = nn(split3(norms[:, R:R + S]), turn)
        turn = onehot(lane == lax.div(src, G) * 2 * G + (1 - core) * G + (src & (G - 1)))
        moved = moved + nn(split3(norms[:, R + S:]), turn)
        score_ref[:, R:] = moved[0:1, :] + moved[1:2, :] + moved[2:3, :]
        put_scores.start()

    for it in range(ITERS):
        if it:
            pl.loop(0, own_steps + 2)(expectation)
        totals = reduce_scatter(fill_sums)
        squares = [jnp.sum(t * t, axis=-1, keepdims=True) for t in totals]
        length = jnp.maximum(jnp.sqrt(squares[0] + squares[1]), 1.0)
        all_gather([(t / length).astype(BF16) for t in totals], place_scores if it == ITERS - 1 else None)
        sent(0)
        sent(1)
    puts = [
        pltpu.make_async_copy(centres.at[h], cent_hbm.at[:, pl.ds(h * Dh, Dh)], load_sem.at[1 + h])
        for h in range(2)
    ]
    for put in puts:
        put.start()
    for put in puts:
        put.wait()
    put_scores.wait()

    wait_send(0, send_a.at[pl.ds(0, S - G)])
    wait_send(1, send_b.at[pl.ds(0, S - Z)])
    wait_send(2, mark_s.at[pl.ds(0, C - 1)])
    wait_send(5, rows.at[pl.ds(0, S)])
    wait_send(6, mark_3.at[pl.ds(0, G - 1)])
    wait_send(8, rows.at[pl.ds(0, S - Z)])


def shards(embeddings, new_label, dest_member, seed_index, kappa):
    R, D = embeddings.shape
    K = seed_index.shape[1]
    C = lax.axis_size("clusters")
    G = lax.axis_size("group")
    S = C * G // 2
    kb = K // G
    slots = R + 2 * S
    hbm = pl.BlockSpec(memory_space=pltpu.HBM)
    phases = 9
    centroids, score = pl.pallas_call(
        functools.partial(kernel, (C, G, R, D, K)),
        name="refine",
        out_shape=(
            jax.ShapeDtypeStruct((K, D), BF16),
            jax.ShapeDtypeStruct((1, slots), F32),
        ),
        in_specs=[hbm, hbm, hbm, hbm, pl.BlockSpec(memory_space=pltpu.SMEM)],
        out_specs=(hbm, hbm),
        scratch_shapes=[
            pltpu.VMEM((R, D), BF16),
            pltpu.VMEM((1, R), I32),
            pltpu.VMEM((1, R), I32),
            pltpu.VMEM((1, K), I32),
            pltpu.VMEM((1, slots), F32),
            pltpu.VMEM((slots, D), BF16),
            pltpu.VMEM((max(R, K), max(R, K)), BF16),
            pltpu.VMEM((S, D), BF16),
            pltpu.VMEM((S, D), BF16),
            pltpu.VMEM((S, D), BF16),
            pltpu.VMEM((S, D), BF16),
            pltpu.VMEM((S, D), BF16),
            pltpu.VMEM((S, D), BF16),
            pltpu.VMEM((K, slots), BF16),
            pltpu.VMEM((2, K, D // 2), BF16),
            pltpu.VMEM((2, 4, kb, D // 2), BF16),
            pltpu.VMEM((2, 4, kb, D // 2), BF16),
            pltpu.VMEM((2, 4, 2, kb, D // 2), BF16),
            pltpu.VMEM((2, 4, kb, D // 2), BF16),
            pltpu.VMEM((2, 3, kb, D // 2), BF16),
            pltpu.VMEM((2, K, D // 2), BF16),
            pltpu.VMEM((1, slots), F32),
            pltpu.VMEM((1, slots), F32),
            pltpu.VMEM((C, 1, 128), F32),
            pltpu.VMEM((C, 1, 128), F32),
            pltpu.VMEM((G, 1, 128), F32),
            pltpu.VMEM((G, 1, 128), F32),
            pltpu.VMEM((128, 128), F32),
            pltpu.SemaphoreType.DMA((phases,)),
            pltpu.SemaphoreType.DMA((phases,)),
            pltpu.SemaphoreType.DMA((4,)),
            pltpu.SemaphoreType.DMA((2,)),
            pltpu.SemaphoreType.DMA((2, 4, 6)),
            pltpu.SemaphoreType.DMA((2, 3)),
            pltpu.SemaphoreType.DMA((2, 4, 4)),
            pltpu.SemaphoreType.DMA((2, 3)),
        ],
        compiler_params=pltpu.CompilerParams(
            collective_id=0, has_side_effects=True, vmem_limit_bytes=60 * 1024 * 1024
        ),
    )(
        embeddings,
        new_label.reshape(1, R),
        dest_member.reshape(1, R),
        seed_index,
        kappa,
    )
    return centroids, score.reshape(slots)


def solution(mesh):
    return jax.shard_map(
        shards,
        mesh=mesh,
        in_specs=(
            P(("clusters", "group"), None),
            P(("clusters", "group")),
            P(("clusters", "group")),
            P("clusters", None),
            P("clusters"),
        ),
        out_specs=(P("clusters", None), P(("clusters", "group"))),
        check_vma=False,
    )
```

```python
import functools

import jax
import jax.numpy as jnp
from jax import lax
from jax.experimental import pallas as pl
from jax.experimental.pallas import tpu as pltpu
from jax.sharding import PartitionSpec as P

ITERS = 2
EPSILON = 1e-06
MESH = pl.DeviceIdType.MESH
F32 = jnp.float32
BF16 = jnp.bfloat16
I32 = jnp.int32


def iota(shape, dim):
    return lax.broadcasted_iota(I32, shape, dim)


def onehot(cond):
    return jnp.where(cond, 1.0, 0.0).astype(BF16)


def nn(a, b):
    return lax.dot_general(a, b, (((1,), (0,)), ((), ())), preferred_element_type=F32)


def nt(a, b):
    return lax.dot_general(a, b, (((1,), (1,)), ((), ())), preferred_element_type=F32)


def tn(a, b):
    return lax.dot_general(a, b, (((0,), (0,)), ((), ())), preferred_element_type=F32)


def rows_at(index, size):
    return pl.ds(pl.multiple_of(index * size, size), size)


def split3(v):
    hi = v.astype(BF16)
    rest = v - hi.astype(F32)
    mid = rest.astype(BF16)
    low = (rest - mid.astype(F32)).astype(BF16)
    pad = jnp.zeros((13,) + v.shape[1:], F32)
    return jnp.concatenate([hi.astype(F32), mid.astype(F32), low.astype(F32), pad], axis=0).astype(BF16)


def kernel(
    dims,
    x_hbm, label_hbm, member_hbm, seed_hbm, kappa_hbm,
    cent_ref, score_ref,
    x_ref, label_ref, member_ref, seed_ref, kappa_ref,
    rows, hot, send_a, send_b, mid_a, mid_b, fwd_a, fwd_b,
    weights, part, relay, combined, nearer, line, line_in, centres, alive, norms,
    mark_s, mark_1, mark_2, mark_3, flat,
    send_sem, recv_sem, load_sem, ready, plane_send, rs_sem, rs_line_sem, ag_sem, ag_line_sem,
):
    C, G, R, D, K = dims
    Z = C // 2
    S = Z * G
    kb = K // G
    c = lax.axis_index("clusters")
    g = lax.axis_index("group")
    z = c // 2
    core = lax.rem(c, 2)

    barrier = pltpu.get_barrier_semaphore()
    for i in range(1, Z):
        pl.semaphore_signal(barrier, inc=1, device_id=(lax.rem(z + i, Z) * 2 + core, g), device_id_type=MESH)
    for i in range(1, G):
        pl.semaphore_signal(barrier, inc=1, device_id=(c, lax.rem(g + i, G)), device_id_type=MESH)

    @pl.when(core == 0)
    def _():
        for i in range(Z):
            pl.semaphore_signal(barrier, inc=1, device_id=(lax.rem(z + i, Z) * 2 + 1, g), device_id_type=MESH)

    chunks = 4
    rstep = R // chunks
    loads = [
        pltpu.make_async_copy(x_hbm.at[pl.ds(i * rstep, rstep)], x_ref.at[pl.ds(i * rstep, rstep)], load_sem.at[4 + i])
        for i in range(chunks)
    ]
    small = [
        pltpu.make_async_copy(src, dst, load_sem.at[i])
        for i, (src, dst) in enumerate(((label_hbm, label_ref), (member_hbm, member_ref), (seed_hbm, seed_ref), (kappa_hbm, kappa_ref)))
    ]
    for load in loads + small:
        load.start()

    def send(phase, src, dst, device):
        pltpu.make_async_remote_copy(
            src_ref=src, dst_ref=dst, send_sem=send_sem.at[phase], recv_sem=recv_sem.at[phase],
            device_id=device, device_id_type=MESH,
        ).start()

    def wait_recv(phase, ref):
        pltpu.make_async_copy(ref, ref, recv_sem.at[phase]).wait()

    def wait_send(phase, ref):
        pltpu.make_async_copy(ref, ref, send_sem.at[phase]).wait()

    ncol = min(D, 256)

    def product(dst, dst_rows, lhs, rhs_ref, rhs_rows):
        @pl.loop(0, D // ncol)
        def _(j):
            cols = rows_at(j, ncol)
            dst[dst_rows, cols] = nn(lhs, rhs_ref[rhs_rows, cols]).astype(BF16)

    for i in range(chunks):
        loads[i].wait()
        at = pl.ds(i * rstep, rstep)
        v = x_ref[at, :].astype(F32)
        scale = lax.rsqrt(jnp.sum(v * v, axis=-1, keepdims=True) + EPSILON)
        rows[at, :] = (v * scale).astype(BF16)
    for load in small:
        load.wait()
    label = label_ref[...]
    member = member_ref[...]
    moving = label != c
    lz = lax.shift_right_logical(label, 1)
    side = label & 1
    own = pl.ds(0, R)

    hot[0:S, 0:R] = onehot(iota((S, R), 0) == jnp.where(moving & (side == 0), lz * G + member, -1))
    product(send_a, slice(None), hot[0:S, 0:R], rows, own)

    pl.semaphore_wait(barrier, Z - 1 + G - 1 + core * Z)

    @pl.when(core == 0)
    def _():
        for i in range(1, Z):
            tz = lax.rem(z + i, Z)
            send(0, send_a.at[rows_at(tz, G)], mid_a.at[0, rows_at(z, G)], (tz * 2, g))
        mid_a[0, rows_at(z, G), :] = send_a[rows_at(z, G), :]

    @pl.when(core == 1)
    def _():
        for i in range(Z):
            tz = lax.rem(z + i, Z)
            pl.semaphore_signal(ready, inc=1, device_id=(tz * 2, g), device_id_type=MESH)
            send(3, send_a.at[rows_at(tz, G)], mid_a.at[1, rows_at(z, G)], (tz * 2, g))

    def cross_marks():
        for i in range(Z):
            tc = lax.rem(z + i, Z) * 2 + 1 - core
            send(4, mark_s.at[tc], mark_1.at[c], (tc, g))

    n = round(G ** 0.5)
    hb = kb // 2
    Dh = D // 2
    px, py = g // n, lax.rem(g, n)
    first = (px, py)
    second = (py, px)
    ORDER = (2, 1, 3, 0)

    def at_plane(h, p, o):
        p, o = lax.rem(p + n, n), lax.rem(o + n, n)
        return p * n + o if h == 0 else o * n + p

    def block(h, dp, do):
        return at_plane(h, first[h] + dp, second[h] + do)

    def part_of(b, half=None):
        if half is None:
            return pl.ds(pl.multiple_of(b * kb, kb), kb)
        return pl.ds(pl.multiple_of(b * kb + half * hb, hb), hb)

    def push(phase, src, dst, sem, b):
        pltpu.make_async_remote_copy(
            src_ref=src, dst_ref=dst, send_sem=plane_send.at[phase], recv_sem=sem,
            device_id=(c, b), device_id_type=MESH,
        ).start()

    def landed(ref, sem):
        pltpu.make_async_copy(ref, ref, sem).wait()

    def sent(phase):
        for h in range(2):
            ref = part.at[h, pl.ds(0, (G - 1) * kb)]
            pltpu.make_async_copy(ref, ref, plane_send.at[phase]).wait()

    TOP, LOW = pl.ds(0, hb), pl.ds(hb, hb)

    def reduce_scatter(fill, meanwhile=None):
        for h in range(2):
            fill(h)
            ahead, behind = block(h, 1, 0), block(h, -1, 0)
            for r in ORDER:
                far = block(h, 2, r)
                push(0, part.at[h, part_of(far, 0)], relay.at[h, r, TOP], rs_sem.at[h, r, 0], ahead)
                push(0, part.at[h, part_of(far, 1)], relay.at[h, r, LOW], rs_sem.at[h, r, 1], behind)
            for r in ORDER:
                push(0, part.at[h, part_of(block(h, 1, r), 1)], nearer.at[h, r, 0, LOW], rs_sem.at[h, r, 2], ahead)
                push(0, part.at[h, part_of(block(h, -1, r), 0)], nearer.at[h, r, 1, TOP], rs_sem.at[h, r, 3], behind)
        if meanwhile is not None:
            meanwhile()
        for r in ORDER:
            for h in range(2):
                ahead, behind = block(h, 1, 0), block(h, -1, 0)
                landed(relay.at[h, r, TOP], rs_sem.at[h, r, 0])
                mine = part[h, part_of(block(h, 1, r), 0), :].astype(F32)
                combined[h, r, TOP, :] = (mine + relay[h, r, TOP, :].astype(F32)).astype(BF16)
                push(0, combined.at[h, r, TOP], nearer.at[h, r, 0, TOP], rs_sem.at[h, r, 4], ahead)
                landed(relay.at[h, r, LOW], rs_sem.at[h, r, 1])
                mine = part[h, part_of(block(h, -1, r), 1), :].astype(F32)
                combined[h, r, LOW, :] = (mine + relay[h, r, LOW, :].astype(F32)).astype(BF16)
                push(0, combined.at[h, r, LOW], nearer.at[h, r, 1, LOW], rs_sem.at[h, r, 5], behind)
        for r in ORDER:
            for h in range(2):
                landed(nearer.at[h, r, 0, LOW], rs_sem.at[h, r, 2])
                landed(nearer.at[h, r, 1, TOP], rs_sem.at[h, r, 3])
                landed(nearer.at[h, r, 0, TOP], rs_sem.at[h, r, 4])
                landed(nearer.at[h, r, 1, LOW], rs_sem.at[h, r, 5])
                total = part[h, part_of(block(h, 0, r)), :].astype(F32)
                total = total + nearer[h, r, 0].astype(F32) + nearer[h, r, 1].astype(F32)
                line[h, r] = total.astype(BF16)
                if r:
                    push(0, line.at[h, r], line_in.at[h, r - 1], rs_line_sem.at[h, r - 1], block(h, 0, r))
        totals = []
        for h in range(2):
            total = line[h, 0].astype(F32)
            for r in range(3):
                landed(line_in.at[h, r], rs_line_sem.at[h, r])
                total = total + line_in[h, r].astype(F32)
            totals.append(total)
        return totals

    def all_gather(blocks, meanwhile=None, midway=None):
        own_at = part_of(g)
        for h in range(2):
            centres[h, own_at, :] = blocks[h]

        def along(h, r):
            here = part_of(block(h, 0, r))
            push(1, centres.at[h, here], centres.at[h, here], ag_sem.at[h, r, 0], block(h, 1, 0))
            push(1, centres.at[h, here], centres.at[h, here], ag_sem.at[h, r, 1], block(h, -1, 0))
            if r == 2:
                push(1, centres.at[h, here], centres.at[h, here], ag_sem.at[h, r, 2], block(h, 2, 0))

        def forward(h, r):
            back, front = block(h, -1, r), block(h, 1, r)
            landed(centres.at[h, part_of(back)], ag_sem.at[h, r, 0])
            if r != 2:
                top = part_of(back, 0)
                push(1, centres.at[h, top], centres.at[h, top], ag_sem.at[h, r, 2], block(h, 1, 0))
            landed(centres.at[h, part_of(front)], ag_sem.at[h, r, 1])
            if r != 2:
                low = part_of(front, 1)
                push(1, centres.at[h, low], centres.at[h, low], ag_sem.at[h, r, 3], block(h, -1, 0))

        for h in range(2):
            for r in (1, 3, 2):
                push(1, centres.at[h, own_at], centres.at[h, own_at], ag_line_sem.at[h, r - 1], block(h, 0, r))
        for h in range(2):
            along(h, 0)
        if meanwhile is not None:
            meanwhile()
        for r in (3, 1):
            for h in range(2):
                landed(centres.at[h, part_of(block(h, 0, r))], ag_line_sem.at[h, n - r - 1])
                along(h, r)
        for h in range(2):
            forward(h, 0)
        for h in range(2):
            landed(centres.at[h, part_of(block(h, 0, 2))], ag_line_sem.at[h, 1])
            along(h, 2)
        if midway is not None:
            midway()
        for r in (3, 1, 2):
            for h in range(2):
                forward(h, r)
        for r in (0, 3, 1, 2):
            for h in range(2):
                far = block(h, 2, r)
                if r == 2:
                    landed(centres.at[h, part_of(far)], ag_sem.at[h, r, 2])
                else:
                    landed(centres.at[h, part_of(far, 0)], ag_sem.at[h, r, 2])
                    landed(centres.at[h, part_of(far, 1)], ag_sem.at[h, r, 3])

    hot[0:R, 0:K] = onehot(iota((R, K), 0) + g * R == seed_ref[...])
    hcol = min(Dh, 256)

    def fill_seeds(h):
        @pl.loop(0, Dh // hcol)
        def _(j):
            cols = pl.ds(pl.multiple_of(h * Dh + j * hcol, hcol), hcol)
            part[h, :, rows_at(j, hcol)] = tn(hot[0:R, 0:K], rows[own, cols]).astype(BF16)

    def fill_sums(h):
        @pl.loop(0, Dh // hcol)
        def _(j):
            cols = pl.ds(pl.multiple_of(h * Dh + j * hcol, hcol), hcol)
            part[h, :, rows_at(j, hcol)] = nn(weights[...], rows[:, cols]).astype(BF16)

    def other_rows():
        hot[0:S, 0:R] = onehot(iota((S, R), 0) == jnp.where(moving & (side == 1), member * Z + lz, -1))
        product(send_b, slice(None), hot[0:S, 0:R], rows, own)
        mid_b[rows_at(g, Z), :] = send_b[rows_at(g, Z), :]
        to_cluster = onehot((iota((128, R), 0) == label) & moving)
        to_member = onehot(iota((128, R), 0) == member)
        marks = nt(to_cluster, to_member)
        for i in range(C):
            mark_s[i] = marks[i:i + 1, :]
        mark_1[c] = mark_s[c]
        for i in range(1, Z):
            tc = lax.rem(z + i, Z) * 2 + core
            send(2, mark_s.at[tc], mark_1.at[c], (tc, g))
        pl.when(core == 1)(cross_marks)

    def other_sends():
        for i in range(1, G):
            tg = lax.rem(g + i, G)
            send(1, send_b.at[rows_at(tg, Z)], mid_b.at[rows_at(g, Z)], (c, tg))

        @pl.when(core == 0)
        def _():
            pl.semaphore_wait(ready, Z)
            cross_marks()

    landing = rows.at[pl.ds(pl.multiple_of(R + core * S + z * G, G), G)]

    def other_legs():
        turn_b = onehot((iota((S, S), 0) & (G - 1)) * Z + lax.div(iota((S, S), 0), G) == iota((S, S), 1))
        wait_recv(1, mid_b.at[pl.ds(0, S - Z)])
        product(fwd_b, slice(None), turn_b, mid_b, slice(None))

        @pl.when(core == 1)
        def _():
            for i in range(1, Z):
                tz = lax.rem(z + i, Z)
                send(5, fwd_b.at[rows_at(tz, G)], landing, (tz * 2 + 1, g))
            landing[...] = fwd_b[rows_at(z, G), :]

        @pl.when(core == 0)
        def _():
            for i in range(Z):
                tz = lax.rem(z + i, Z)
                send(6, fwd_b.at[rows_at(tz, G)], landing, (tz * 2 + 1, g))

    first_blocks = [t.astype(BF16) for t in reduce_scatter(fill_seeds, other_rows)]
    all_gather(first_blocks, other_sends, other_legs)
    sent(0)
    sent(1)

    wait_recv(2, mark_s.at[pl.ds(0, Z - 1)])
    wait_recv(4, mark_s.at[pl.ds(0, Z)])
    flat[...] = jnp.zeros_like(flat)
    for i in range(C):
        flat[i:i + 1, :] = mark_1[i]
    eye = onehot(iota((16, 128), 0) == iota((16, 128), 1))
    turned = nt(eye, flat[...].astype(BF16))
    for i in range(G):
        mark_2[i] = turned[i:i + 1, :]
    for i in range(1, G):
        tg = lax.rem(g + i, G)
        send(9, mark_2.at[tg], mark_3.at[g], (c, tg))
    mark_3[g] = mark_2[g]

    turn_a = onehot((iota((S, S), 0) & (Z - 1)) * G + lax.div(iota((S, S), 0), Z) == iota((S, S), 1))

    def second_leg(part_a, phase):
        at = pl.ds(pl.multiple_of(R + part_a * S + g * Z, Z), Z)

        @pl.loop(0, D // ncol)
        def _(j):
            cols = rows_at(j, ncol)
            fwd_a[part_a, :, cols] = nn(turn_a, mid_a[part_a, :, cols]).astype(BF16)

        for i in range(1, G):
            tg = lax.rem(g + i, G)
            send(phase, fwd_a.at[part_a, rows_at(tg, Z)], rows.at[at], (c, tg))
        rows[at, :] = fwd_a[part_a, rows_at(g, Z), :]

    @pl.when(core == 0)
    def _():
        wait_recv(0, mid_a.at[0, pl.ds(0, S - G)])
        second_leg(0, 8)
        wait_recv(3, mid_a.at[1])
        second_leg(1, 7)

    alive[:, 0:R] = jnp.where(moving, 0.0, 1.0)

    def origin(index):
        q = index & (S - 1)
        from_z = (1 - core) * (q & (Z - 1)) + core * lax.div(q, G)
        from_g = (1 - core) * lax.div(q, Z) + core * (q & (G - 1))
        return 2 * from_z + lax.div(index, S), from_g

    kappa = kappa_ref[0]
    step = S

    def expectation(i):
        at = rows_at(i, step)
        scores = nt(centres[0], rows[at, 0:Dh]) + nt(centres[1], rows[at, Dh:D])
        scores = kappa * scores
        largest = jnp.max(scores, axis=0, keepdims=True)
        powered = jnp.exp(scores - largest)
        summed = jnp.sum(powered, axis=0, keepdims=True)
        here = alive[:, at]
        weights[:, at] = (powered * (1.0 / summed) * here).astype(BF16)
        norms[:, at] = (largest + jnp.log(summed)) * here

    own_steps = R // step
    pl.loop(0, own_steps)(expectation)

    wait_recv(9, mark_3.at[pl.ds(0, G - 1)])
    for i in range(G):
        flat[i:i + 1, :] = mark_3[i]
    from_c, from_g = origin(iota((1, 2 * S), 1))
    held = nn(flat[0:16, :].astype(BF16), onehot(iota((128, 2 * S), 0) == from_c))
    alive[:, R:] = jnp.sum(jnp.where(iota((16, 2 * S), 0) == from_g, held, 0.0), axis=0, keepdims=True)

    @pl.when(core == 0)
    def _():
        wait_recv(8, rows.at[pl.ds(0, S - Z)])

    @pl.when(core == 1)
    def _():
        wait_recv(5, rows.at[pl.ds(0, S - G)])

    expectation(own_steps + core)

    @pl.when(core == 0)
    def _():
        wait_recv(7, rows.at[pl.ds(0, S - Z)])

    @pl.when(core == 1)
    def _():
        wait_recv(6, rows.at[pl.ds(0, S)])

    expectation(own_steps + 1 - core)

    def place_scores():
        score_ref[:, 0:R] = norms[:, 0:R]
        from_c, from_g = origin(iota((2 * S, 1), 0))
        turn = onehot(iota((2 * S, 2 * S), 1) == from_c * G + from_g)
        moved = nn(split3(norms[:, R:]), turn)
        score_ref[:, R:] = moved[0:1, :] + moved[1:2, :] + moved[2:3, :]

    for it in range(ITERS):
        if it:
            pl.loop(0, own_steps + 2)(expectation)
        totals = reduce_scatter(fill_sums)
        squares = [jnp.sum(t * t, axis=-1, keepdims=True) for t in totals]
        length = jnp.maximum(jnp.sqrt(squares[0] + squares[1]), 1.0)
        all_gather([(t / length).astype(BF16) for t in totals], place_scores if it == ITERS - 1 else None)
        sent(0)
        sent(1)
    cent_ref[:, 0:Dh] = centres[0]
    cent_ref[:, Dh:D] = centres[1]

    wait_send(1, send_b.at[pl.ds(0, S - Z)])
    wait_send(2, mark_s.at[pl.ds(0, Z - 1)])
    wait_send(4, mark_s.at[pl.ds(0, Z)])
    wait_send(9, mark_3.at[pl.ds(0, G - 1)])

    @pl.when(core == 0)
    def _():
        wait_send(0, send_a.at[pl.ds(0, S - G)])
        wait_send(6, rows.at[pl.ds(0, S)])
        wait_send(7, rows.at[pl.ds(0, S - Z)])
        wait_send(8, rows.at[pl.ds(0, S - Z)])

    @pl.when(core == 1)
    def _():
        wait_send(3, rows.at[pl.ds(0, S)])
        wait_send(5, rows.at[pl.ds(0, S - G)])


def shards(embeddings, new_label, dest_member, seed_index, kappa):
    R, D = embeddings.shape
    K = seed_index.shape[1]
    C = lax.axis_size("clusters")
    G = lax.axis_size("group")
    S = C * G // 2
    kb = K // G
    slots = R + 2 * S
    hbm = pl.BlockSpec(memory_space=pltpu.HBM)
    vmem = pl.BlockSpec(memory_space=pltpu.VMEM)
    phases = 10
    centroids, score = pl.pallas_call(
        functools.partial(kernel, (C, G, R, D, K)),
        name="refine",
        out_shape=(
            pltpu.VMEM((K, D), BF16),
            pltpu.VMEM((1, slots), F32),
        ),
        in_specs=[hbm] * 5,
        out_specs=(vmem, vmem),
        scratch_shapes=[
            pltpu.VMEM((R, D), BF16),
            pltpu.VMEM((1, R), I32),
            pltpu.VMEM((1, R), I32),
            pltpu.VMEM((1, K), I32),
            pltpu.SMEM((1,), F32),
            pltpu.VMEM((slots, D), BF16),
            pltpu.VMEM((max(R, K), max(R, K)), BF16),
            pltpu.VMEM((S, D), BF16),
            pltpu.VMEM((S, D), BF16),
            pltpu.VMEM((2, S, D), BF16),
            pltpu.VMEM((S, D), BF16),
            pltpu.VMEM((2, S, D), BF16),
            pltpu.VMEM((S, D), BF16),
            pltpu.VMEM((K, slots), BF16),
            pltpu.VMEM((2, K, D // 2), BF16),
            pltpu.VMEM((2, 4, kb, D // 2), BF16),
            pltpu.VMEM((2, 4, kb, D // 2), BF16),
            pltpu.VMEM((2, 4, 2, kb, D // 2), BF16),
            pltpu.VMEM((2, 4, kb, D // 2), BF16),
            pltpu.VMEM((2, 3, kb, D // 2), BF16),
            pltpu.VMEM((2, K, D // 2), BF16),
            pltpu.VMEM((1, slots), F32),
            pltpu.VMEM((1, slots), F32),
            pltpu.VMEM((C, 1, 128), F32),
            pltpu.VMEM((C, 1, 128), F32),
            pltpu.VMEM((G, 1, 128), F32),
            pltpu.VMEM((G, 1, 128), F32),
            pltpu.VMEM((128, 128), F32),
            pltpu.SemaphoreType.DMA((phases,)),
            pltpu.SemaphoreType.DMA((phases,)),
            pltpu.SemaphoreType.DMA((8,)),
            pltpu.SemaphoreType.REGULAR,
            pltpu.SemaphoreType.DMA((2,)),
            pltpu.SemaphoreType.DMA((2, 4, 6)),
            pltpu.SemaphoreType.DMA((2, 3)),
            pltpu.SemaphoreType.DMA((2, 4, 4)),
            pltpu.SemaphoreType.DMA((2, 3)),
        ],
        compiler_params=pltpu.CompilerParams(
            collective_id=0, has_side_effects=True, vmem_limit_bytes=60 * 1024 * 1024
        ),
    )(
        embeddings,
        new_label.reshape(1, R),
        dest_member.reshape(1, R),
        seed_index,
        kappa,
    )
    return centroids, score.reshape(slots)


def solution(mesh):
    return jax.shard_map(
        shards,
        mesh=mesh,
        in_specs=(
            P(("clusters", "group"), None),
            P(("clusters", "group")),
            P(("clusters", "group")),
            P("clusters", None),
            P("clusters"),
        ),
        out_specs=(P("clusters", None), P(("clusters", "group"))),
        check_vma=False,
    )
```

```python
import functools

import jax
import jax.numpy as jnp
from jax import lax
from jax.experimental import pallas as pl
from jax.experimental.pallas import tpu as pltpu
from jax.sharding import PartitionSpec as P

ITERS = 2
EPSILON = 1e-06
MESH = pl.DeviceIdType.MESH
F32 = jnp.float32
BF16 = jnp.bfloat16
I32 = jnp.int32


def iota(shape, dim):
    return lax.broadcasted_iota(I32, shape, dim)


def onehot(cond):
    return jnp.where(cond, 1.0, 0.0).astype(BF16)


def nn(a, b):
    return lax.dot_general(a, b, (((1,), (0,)), ((), ())), preferred_element_type=F32)


def nt(a, b):
    return lax.dot_general(a, b, (((1,), (1,)), ((), ())), preferred_element_type=F32)


def tn(a, b):
    return lax.dot_general(a, b, (((0,), (0,)), ((), ())), preferred_element_type=F32)


def rows_at(index, size):
    if isinstance(index, int):
        return pl.ds(index * size, size)
    return pl.ds(pl.multiple_of(index * size, size), size)


def split3(v):
    hi = v.astype(BF16)
    rest = v - hi.astype(F32)
    mid = rest.astype(BF16)
    low = (rest - mid.astype(F32)).astype(BF16)
    pad = jnp.zeros((13,) + v.shape[1:], F32)
    return jnp.concatenate([hi.astype(F32), mid.astype(F32), low.astype(F32), pad], axis=0).astype(BF16)


def kernel(
    dims,
    x_hbm, label_hbm, member_hbm, seed_hbm, kappa_hbm,
    cent_ref, score_ref,
    x_ref, label_ref, member_ref, seed_ref, kappa_ref,
    rows, hot, send_a, send_b, mid_a, mid_b, fwd_a, fwd_b,
    weights, part, relay, combined, nearer, line, line_in, centres, alive, norms,
    mark_s, mark_1, mark_2, mark_3, flat,
    send_sem, recv_sem, load_sem, ready, plane_send, rs_sem, rs_line_sem, ag_sem, ag_line_sem,
):
    C, G, R, D, K = dims
    Z = C // 2
    S = Z * G
    kb = K // G
    c = lax.axis_index("clusters")
    g = lax.axis_index("group")
    z = c // 2
    core = lax.rem(c, 2)

    chunks = 4
    rstep = R // chunks
    loads = [
        pltpu.make_async_copy(x_hbm.at[pl.ds(i * rstep, rstep)], x_ref.at[pl.ds(i * rstep, rstep)], load_sem.at[4 + i])
        for i in range(chunks)
    ]
    small = [
        pltpu.make_async_copy(src, dst, load_sem.at[i])
        for i, (src, dst) in enumerate(((label_hbm, label_ref), (member_hbm, member_ref), (seed_hbm, seed_ref), (kappa_hbm, kappa_ref)))
    ]
    for load in loads + small:
        load.start()

    barrier = pltpu.get_barrier_semaphore()
    for i in range(1, Z):
        pl.semaphore_signal(barrier, inc=1, device_id=(lax.rem(z + i, Z) * 2 + core, g), device_id_type=MESH)
    for i in range(1, G):
        pl.semaphore_signal(barrier, inc=1, device_id=(c, lax.rem(g + i, G)), device_id_type=MESH)

    @pl.when(core == 0)
    def _():
        for i in range(Z):
            pl.semaphore_signal(barrier, inc=1, device_id=(lax.rem(z + i, Z) * 2 + 1, g), device_id_type=MESH)

    def send(phase, src, dst, device):
        pltpu.make_async_remote_copy(
            src_ref=src, dst_ref=dst, send_sem=send_sem.at[phase], recv_sem=recv_sem.at[phase],
            device_id=device, device_id_type=MESH,
        ).start()

    def wait_recv(phase, ref):
        pltpu.make_async_copy(ref, ref, recv_sem.at[phase]).wait()

    def wait_send(phase, ref):
        pltpu.make_async_copy(ref, ref, send_sem.at[phase]).wait()

    ncol = min(D, 256)

    def product(dst, dst_rows, lhs, rhs_ref, rhs_rows):
        @pl.loop(0, D // ncol)
        def _(j):
            cols = rows_at(j, ncol)
            dst[dst_rows, cols] = nn(lhs, rhs_ref[rhs_rows, cols]).astype(BF16)

    FAR = sorted(range(1, Z), key=lambda i: -min(i, Z - i))

    for i in range(chunks):
        loads[i].wait()
        at = pl.ds(i * rstep, rstep)
        v = x_ref[at, :].astype(F32)
        scale = lax.rsqrt(jnp.sum(v * v, axis=-1, keepdims=True) + EPSILON)
        rows[at, :] = (v * scale).astype(BF16)
    for load in small:
        load.wait()
    label = label_ref[...]
    member = member_ref[...]
    moving = label != c
    lz = lax.shift_right_logical(label, 1)
    side = label & 1
    own = pl.ds(0, R)

    hot[0:S, 0:R] = onehot(iota((S, R), 0) == jnp.where(moving & (side == 0), lz * G + member, -1))
    product(send_a, slice(None), hot[0:S, 0:R], rows, own)

    to_cluster = onehot((iota((128, R), 0) == label) & moving)
    to_member = onehot(iota((128, R), 0) == member)
    marks = nt(to_cluster, to_member)
    for i in range(C):
        mark_s[i] = marks[i:i + 1, :]
    mark_1[c] = mark_s[c]

    def cross_marks():
        for i in range(Z):
            tc = lax.rem(z + i, Z) * 2 + 1 - core
            send(4, mark_s.at[tc], mark_1.at[c], (tc, g))

    pl.semaphore_wait(barrier, Z - 1 + G - 1 + core * Z)
    for i in range(1, Z):
        tc = lax.rem(z + i, Z) * 2 + core
        send(2, mark_s.at[tc], mark_1.at[c], (tc, g))
    pl.when(core == 1)(cross_marks)

    @pl.when(core == 0)
    def _():
        for i in FAR:
            tz = lax.rem(z + i, Z)
            send(0, send_a.at[rows_at(tz, G)], mid_a.at[0, rows_at(z, G)], (tz * 2, g))
        mid_a[0, rows_at(z, G), :] = send_a[rows_at(z, G), :]

    @pl.when(core == 1)
    def _():
        for i in FAR + [0]:
            tz = lax.rem(z + i, Z)
            pl.semaphore_signal(ready, inc=1, device_id=(tz * 2, g), device_id_type=MESH)
            send(3, send_a.at[rows_at(tz, G)], mid_a.at[1, rows_at(z, G)], (tz * 2, g))

    n = round(G ** 0.5)
    hb = kb // 2
    Dh = D // 2
    px, py = g // n, lax.rem(g, n)
    first = (px, py)
    second = (py, px)
    ORDER = (2, 1, 3, 0)

    def at_plane(h, p, o):
        p, o = lax.rem(p + n, n), lax.rem(o + n, n)
        return p * n + o if h == 0 else o * n + p

    def block(h, dp, do):
        return at_plane(h, first[h] + dp, second[h] + do)

    def part_of(b, half=None):
        if half is None:
            return pl.ds(pl.multiple_of(b * kb, kb), kb)
        return pl.ds(pl.multiple_of(b * kb + half * hb, hb), hb)

    def push(phase, src, dst, sem, b):
        pltpu.make_async_remote_copy(
            src_ref=src, dst_ref=dst, send_sem=plane_send.at[phase], recv_sem=sem,
            device_id=(c, b), device_id_type=MESH,
        ).start()

    def landed(ref, sem):
        pltpu.make_async_copy(ref, ref, sem).wait()

    def sent(phase):
        for h in range(2):
            ref = part.at[h, pl.ds(0, (G - 1) * kb)]
            pltpu.make_async_copy(ref, ref, plane_send.at[phase]).wait()

    TOP, LOW = pl.ds(0, hb), pl.ds(hb, hb)

    def reduce_scatter(fill, meanwhile=None):
        for h in range(2):
            fill(h)
            ahead, behind = block(h, 1, 0), block(h, -1, 0)
            for r in ORDER:
                far = block(h, 2, r)
                push(0, part.at[h, part_of(far, 0)], relay.at[h, r, TOP], rs_sem.at[h, r, 0], ahead)
                push(0, part.at[h, part_of(far, 1)], relay.at[h, r, LOW], rs_sem.at[h, r, 1], behind)
            for r in ORDER:
                push(0, part.at[h, part_of(block(h, 1, r), 1)], nearer.at[h, r, 0, LOW], rs_sem.at[h, r, 2], ahead)
                push(0, part.at[h, part_of(block(h, -1, r), 0)], nearer.at[h, r, 1, TOP], rs_sem.at[h, r, 3], behind)
        if meanwhile is not None:
            meanwhile()
        for r in ORDER:
            for h in range(2):
                ahead, behind = block(h, 1, 0), block(h, -1, 0)
                landed(relay.at[h, r, TOP], rs_sem.at[h, r, 0])
                mine = part[h, part_of(block(h, 1, r), 0), :].astype(F32)
                combined[h, r, TOP, :] = (mine + relay[h, r, TOP, :].astype(F32)).astype(BF16)
                push(0, combined.at[h, r, TOP], nearer.at[h, r, 0, TOP], rs_sem.at[h, r, 4], ahead)
                landed(relay.at[h, r, LOW], rs_sem.at[h, r, 1])
                mine = part[h, part_of(block(h, -1, r), 1), :].astype(F32)
                combined[h, r, LOW, :] = (mine + relay[h, r, LOW, :].astype(F32)).astype(BF16)
                push(0, combined.at[h, r, LOW], nearer.at[h, r, 1, LOW], rs_sem.at[h, r, 5], behind)
        for r in ORDER:
            for h in range(2):
                landed(nearer.at[h, r, 0, LOW], rs_sem.at[h, r, 2])
                landed(nearer.at[h, r, 1, TOP], rs_sem.at[h, r, 3])
                landed(nearer.at[h, r, 0, TOP], rs_sem.at[h, r, 4])
                landed(nearer.at[h, r, 1, LOW], rs_sem.at[h, r, 5])
                total = part[h, part_of(block(h, 0, r)), :].astype(F32)
                total = total + nearer[h, r, 0].astype(F32) + nearer[h, r, 1].astype(F32)
                line[h, r] = total.astype(BF16)
                if r:
                    push(0, line.at[h, r], line_in.at[h, r - 1], rs_line_sem.at[h, r - 1], block(h, 0, r))
        totals = []
        for h in range(2):
            total = line[h, 0].astype(F32)
            for r in range(3):
                landed(line_in.at[h, r], rs_line_sem.at[h, r])
                total = total + line_in[h, r].astype(F32)
            totals.append(total)
        return totals

    def all_gather(blocks, meanwhile=None, midway=None):
        own_at = part_of(g)
        for h in range(2):
            centres[h, own_at, :] = blocks[h]

        def along(h, r):
            here = part_of(block(h, 0, r))
            push(1, centres.at[h, here], centres.at[h, here], ag_sem.at[h, r, 0], block(h, 1, 0))
            push(1, centres.at[h, here], centres.at[h, here], ag_sem.at[h, r, 1], block(h, -1, 0))
            if r == 2:
                push(1, centres.at[h, here], centres.at[h, here], ag_sem.at[h, r, 2], block(h, 2, 0))

        def forward(h, r):
            back, front = block(h, -1, r), block(h, 1, r)
            landed(centres.at[h, part_of(back)], ag_sem.at[h, r, 0])
            if r != 2:
                top = part_of(back, 0)
                push(1, centres.at[h, top], centres.at[h, top], ag_sem.at[h, r, 2], block(h, 1, 0))
            landed(centres.at[h, part_of(front)], ag_sem.at[h, r, 1])
            if r != 2:
                low = part_of(front, 1)
                push(1, centres.at[h, low], centres.at[h, low], ag_sem.at[h, r, 3], block(h, -1, 0))

        for h in range(2):
            for r in (1, 3, 2):
                push(1, centres.at[h, own_at], centres.at[h, own_at], ag_line_sem.at[h, r - 1], block(h, 0, r))
        for h in range(2):
            along(h, 0)
        if meanwhile is not None:
            meanwhile()
        for r in (3, 1):
            for h in range(2):
                landed(centres.at[h, part_of(block(h, 0, r))], ag_line_sem.at[h, n - r - 1])
                along(h, r)
        for h in range(2):
            forward(h, 0)
        for h in range(2):
            landed(centres.at[h, part_of(block(h, 0, 2))], ag_line_sem.at[h, 1])
            along(h, 2)
        if midway is not None:
            midway()
        for r in (3, 1, 2):
            for h in range(2):
                forward(h, r)
        for r in (0, 3, 1, 2):
            for h in range(2):
                far = block(h, 2, r)
                if r == 2:
                    landed(centres.at[h, part_of(far)], ag_sem.at[h, r, 2])
                else:
                    landed(centres.at[h, part_of(far, 0)], ag_sem.at[h, r, 2])
                    landed(centres.at[h, part_of(far, 1)], ag_sem.at[h, r, 3])

    hot[0:R, 0:K] = onehot(iota((R, K), 0) + g * R == seed_ref[...])
    hcol = min(Dh, 256)

    def fill_seeds(h):
        @pl.loop(0, Dh // hcol)
        def _(j):
            cols = pl.ds(pl.multiple_of(h * Dh + j * hcol, hcol), hcol)
            part[h, :, rows_at(j, hcol)] = tn(hot[0:R, 0:K], rows[own, cols]).astype(BF16)

    def fill_sums(h):
        @pl.loop(0, Dh // hcol)
        def _(j):
            cols = pl.ds(pl.multiple_of(h * Dh + j * hcol, hcol), hcol)
            part[h, :, rows_at(j, hcol)] = nn(weights[...], rows[:, cols]).astype(BF16)

    def other_rows():
        hot[0:S, 0:R] = onehot(iota((S, R), 0) == jnp.where(moving & (side == 1), member * Z + lz, -1))
        product(send_b, slice(None), hot[0:S, 0:R], rows, own)
        mid_b[rows_at(g, Z), :] = send_b[rows_at(g, Z), :]

    def other_sends():
        for i in range(1, G):
            tg = lax.rem(g + i, G)
            send(1, send_b.at[rows_at(tg, Z)], mid_b.at[rows_at(g, Z)], (c, tg))

        @pl.when(core == 0)
        def _():
            pl.semaphore_wait(ready, Z)
            cross_marks()

    landing = rows.at[pl.ds(pl.multiple_of(R + core * S + z * G, G), G)]

    def other_legs():
        turn_b = onehot((iota((S, S), 0) & (G - 1)) * Z + lax.div(iota((S, S), 0), G) == iota((S, S), 1))
        wait_recv(1, mid_b.at[pl.ds(0, S - Z)])
        product(fwd_b, slice(None), turn_b, mid_b, slice(None))

        @pl.when(core == 1)
        def _():
            for i in FAR:
                tz = lax.rem(z + i, Z)
                send(5, fwd_b.at[rows_at(tz, G)], landing, (tz * 2 + 1, g))
            landing[...] = fwd_b[rows_at(z, G), :]

        @pl.when(core == 0)
        def _():
            for i in FAR + [0]:
                tz = lax.rem(z + i, Z)
                send(6, fwd_b.at[rows_at(tz, G)], landing, (tz * 2 + 1, g))

    first_blocks = [t.astype(BF16) for t in reduce_scatter(fill_seeds, other_rows)]
    all_gather(first_blocks, other_sends, other_legs)
    sent(0)
    sent(1)

    wait_recv(2, mark_s.at[pl.ds(0, Z - 1)])
    wait_recv(4, mark_s.at[pl.ds(0, Z)])
    flat[...] = jnp.zeros_like(flat)
    for i in range(C):
        flat[i:i + 1, :] = mark_1[i]
    eye = onehot(iota((16, 128), 0) == iota((16, 128), 1))
    turned = nt(eye, flat[...].astype(BF16))
    for i in range(G):
        mark_2[i] = turned[i:i + 1, :]
    for i in range(1, G):
        tg = lax.rem(g + i, G)
        send(9, mark_2.at[tg], mark_3.at[g], (c, tg))
    mark_3[g] = mark_2[g]

    turn_a = onehot((iota((S, S), 0) & (Z - 1)) * G + lax.div(iota((S, S), 0), Z) == iota((S, S), 1))

    def second_leg(part_a, phase):
        at = pl.ds(pl.multiple_of(R + part_a * S + g * Z, Z), Z)

        @pl.loop(0, D // ncol)
        def _(j):
            cols = rows_at(j, ncol)
            fwd_a[part_a, :, cols] = nn(turn_a, mid_a[part_a, :, cols]).astype(BF16)

        for i in range(1, G):
            tg = lax.rem(g + i, G)
            send(phase, fwd_a.at[part_a, rows_at(tg, Z)], rows.at[at], (c, tg))
        rows[at, :] = fwd_a[part_a, rows_at(g, Z), :]

    @pl.when(core == 0)
    def _():
        wait_recv(0, mid_a.at[0, pl.ds(0, S - G)])
        second_leg(0, 8)
        wait_recv(3, mid_a.at[1])
        second_leg(1, 7)

    alive[:, 0:R] = jnp.where(moving, 0.0, 1.0)

    def origin(index):
        q = index & (S - 1)
        from_z = (1 - core) * (q & (Z - 1)) + core * lax.div(q, G)
        from_g = (1 - core) * lax.div(q, Z) + core * (q & (G - 1))
        return 2 * from_z + lax.div(index, S), from_g

    kappa = kappa_ref[0, 0]
    step = S

    def expectation(i):
        at = rows_at(i, step)
        scores = nt(centres[0], rows[at, 0:Dh]) + nt(centres[1], rows[at, Dh:D])
        scores = kappa * scores
        largest = jnp.max(scores, axis=0, keepdims=True)
        powered = jnp.exp(scores - largest)
        summed = jnp.sum(powered, axis=0, keepdims=True)
        here = alive[:, at]
        weights[:, at] = (powered * (1.0 / summed) * here).astype(BF16)
        norms[:, at] = (largest + jnp.log(summed)) * here

    own_steps = R // step
    pl.loop(0, own_steps)(expectation)

    wait_recv(9, mark_3.at[pl.ds(0, G - 1)])
    for i in range(G):
        flat[i:i + 1, :] = mark_3[i]
    from_c, from_g = origin(iota((1, 2 * S), 1))
    held = nn(flat[0:16, :].astype(BF16), onehot(iota((128, 2 * S), 0) == from_c))
    alive[:, R:] = jnp.sum(jnp.where(iota((16, 2 * S), 0) == from_g, held, 0.0), axis=0, keepdims=True)

    @pl.when(core == 0)
    def _():
        wait_recv(8, rows.at[pl.ds(0, S - Z)])

    @pl.when(core == 1)
    def _():
        wait_recv(5, rows.at[pl.ds(0, S - G)])

    expectation(own_steps + core)

    @pl.when(core == 0)
    def _():
        wait_recv(7, rows.at[pl.ds(0, S - Z)])

    @pl.when(core == 1)
    def _():
        wait_recv(6, rows.at[pl.ds(0, S)])

    expectation(own_steps + 1 - core)

    def place_scores():
        score_ref[:, 0:R] = norms[:, 0:R]
        from_c, from_g = origin(iota((2 * S, 1), 0))
        turn = onehot(iota((2 * S, 2 * S), 1) == from_c * G + from_g)
        moved = nn(split3(norms[:, R:]), turn)
        score_ref[:, R:] = moved[0:1, :] + moved[1:2, :] + moved[2:3, :]

    for it in range(ITERS):
        if it:
            for i in range(own_steps + 2):
                expectation(i)
        totals = reduce_scatter(fill_sums)
        squares = [jnp.sum(t * t, axis=-1, keepdims=True) for t in totals]
        length = jnp.maximum(jnp.sqrt(squares[0] + squares[1]), 1.0)
        all_gather([(t / length).astype(BF16) for t in totals], place_scores if it == ITERS - 1 else None)
        sent(0)
        sent(1)
    cent_ref[:, 0:Dh] = centres[0]
    cent_ref[:, Dh:D] = centres[1]

    wait_send(1, send_b.at[pl.ds(0, S - Z)])
    wait_send(2, mark_s.at[pl.ds(0, Z - 1)])
    wait_send(4, mark_s.at[pl.ds(0, Z)])
    wait_send(9, mark_3.at[pl.ds(0, G - 1)])

    @pl.when(core == 0)
    def _():
        wait_send(0, send_a.at[pl.ds(0, S - G)])
        wait_send(6, rows.at[pl.ds(0, S)])
        wait_send(7, rows.at[pl.ds(0, S - Z)])
        wait_send(8, rows.at[pl.ds(0, S - Z)])

    @pl.when(core == 1)
    def _():
        wait_send(3, rows.at[pl.ds(0, S)])
        wait_send(5, rows.at[pl.ds(0, S - G)])


def shards(embeddings, new_label, dest_member, seed_index, kappa):
    R, D = embeddings.shape
    K = seed_index.shape[1]
    C = lax.axis_size("clusters")
    G = lax.axis_size("group")
    S = C * G // 2
    kb = K // G
    slots = R + 2 * S
    hbm = pl.BlockSpec(memory_space=pltpu.HBM)
    vmem = pl.BlockSpec(memory_space=pltpu.VMEM)
    phases = 10
    centroids, score = pl.pallas_call(
        functools.partial(kernel, (C, G, R, D, K)),
        name="refine",
        out_shape=(
            pltpu.VMEM((K, D), BF16),
            pltpu.VMEM((1, slots), F32),
        ),
        in_specs=[hbm] * 5,
        out_specs=(vmem, vmem),
        scratch_shapes=[
            pltpu.VMEM((R, D), BF16),
            pltpu.VMEM((1, R), I32),
            pltpu.VMEM((1, R), I32),
            pltpu.VMEM((1, K), I32),
            pltpu.SMEM((1, 1), F32),
            pltpu.VMEM((slots, D), BF16),
            pltpu.VMEM((max(R, K), max(R, K)), BF16),
            pltpu.VMEM((S, D), BF16),
            pltpu.VMEM((S, D), BF16),
            pltpu.VMEM((2, S, D), BF16),
            pltpu.VMEM((S, D), BF16),
            pltpu.VMEM((2, S, D), BF16),
            pltpu.VMEM((S, D), BF16),
            pltpu.VMEM((K, slots), BF16),
            pltpu.VMEM((2, K, D // 2), BF16),
            pltpu.VMEM((2, 4, kb, D // 2), BF16),
            pltpu.VMEM((2, 4, kb, D // 2), BF16),
            pltpu.VMEM((2, 4, 2, kb, D // 2), BF16),
            pltpu.VMEM((2, 4, kb, D // 2), BF16),
            pltpu.VMEM((2, 3, kb, D // 2), BF16),
            pltpu.VMEM((2, K, D // 2), BF16),
            pltpu.VMEM((1, slots), F32),
            pltpu.VMEM((1, slots), F32),
            pltpu.VMEM((C, 1, 128), F32),
            pltpu.VMEM((C, 1, 128), F32),
            pltpu.VMEM((G, 1, 128), F32),
            pltpu.VMEM((G, 1, 128), F32),
            pltpu.VMEM((128, 128), F32),
            pltpu.SemaphoreType.DMA((phases,)),
            pltpu.SemaphoreType.DMA((phases,)),
            pltpu.SemaphoreType.DMA((8,)),
            pltpu.SemaphoreType.REGULAR,
            pltpu.SemaphoreType.DMA((2,)),
            pltpu.SemaphoreType.DMA((2, 4, 6)),
            pltpu.SemaphoreType.DMA((2, 3)),
            pltpu.SemaphoreType.DMA((2, 4, 4)),
            pltpu.SemaphoreType.DMA((2, 3)),
        ],
        compiler_params=pltpu.CompilerParams(
            collective_id=0, has_side_effects=True, vmem_limit_bytes=60 * 1024 * 1024
        ),
    )(
        embeddings,
        new_label.reshape(1, R),
        dest_member.reshape(1, R),
        seed_index,
        kappa.reshape(1, 1),
    )
    return centroids, score.reshape(slots)


def solution(mesh):
    return jax.shard_map(
        shards,
        mesh=mesh,
        in_specs=(
            P(("clusters", "group"), None),
            P(("clusters", "group")),
            P(("clusters", "group")),
            P("clusters", None),
            P("clusters"),
        ),
        out_specs=(P("clusters", None), P(("clusters", "group"))),
        check_vma=False,
    )
```

```python
import functools

import jax
import jax.numpy as jnp
from jax import lax
from jax.experimental import pallas as pl
from jax.experimental.pallas import tpu as pltpu
from jax.sharding import PartitionSpec as P

ITERS = 2
EPSILON = 1e-06
MESH = pl.DeviceIdType.MESH
F32 = jnp.float32
BF16 = jnp.bfloat16
I32 = jnp.int32


def iota(shape, dim):
    return lax.broadcasted_iota(I32, shape, dim)


def onehot(cond):
    return jnp.where(cond, 1.0, 0.0).astype(BF16)


def nn(a, b):
    return lax.dot_general(a, b, (((1,), (0,)), ((), ())), preferred_element_type=F32)


def nt(a, b):
    return lax.dot_general(a, b, (((1,), (1,)), ((), ())), preferred_element_type=F32)


def tn(a, b):
    return lax.dot_general(a, b, (((0,), (0,)), ((), ())), preferred_element_type=F32)


def rows_at(index, size):
    if isinstance(index, int):
        return pl.ds(index * size, size)
    return pl.ds(pl.multiple_of(index * size, size), size)


def split3(v):
    hi = v.astype(BF16)
    rest = v - hi.astype(F32)
    mid = rest.astype(BF16)
    low = (rest - mid.astype(F32)).astype(BF16)
    pad = jnp.zeros((13,) + v.shape[1:], F32)
    return jnp.concatenate([hi.astype(F32), mid.astype(F32), low.astype(F32), pad], axis=0).astype(BF16)


def kernel(
    dims,
    x_hbm, label_hbm, member_hbm, seed_hbm, kappa_hbm,
    cent_ref, score_ref,
    x_ref, label_ref, member_ref, seed_ref, kappa_ref,
    rows, hot, send_a, send_b, mid_a, mid_b, fwd_a, fwd_b,
    weights, part, relay, combined, nearer, line, line_in, centres, alive, norms,
    mark_s, mark_1, mark_2, mark_3, flat,
    send_sem, recv_sem, load_sem, ready, plane_send, rs_sem, rs_line_sem, ag_sem, ag_line_sem,
):
    C, G, R, D, K = dims
    Z = C // 2
    S = Z * G
    kb = K // G
    c = lax.axis_index("clusters")
    g = lax.axis_index("group")
    z = c // 2
    core = lax.rem(c, 2)

    chunks = 4
    rstep = R // chunks
    loads = [
        pltpu.make_async_copy(x_hbm.at[pl.ds(i * rstep, rstep)], x_ref.at[pl.ds(i * rstep, rstep)], load_sem.at[4 + i])
        for i in range(chunks)
    ]
    small = [
        pltpu.make_async_copy(src, dst, load_sem.at[i])
        for i, (src, dst) in enumerate(((label_hbm, label_ref), (member_hbm, member_ref), (seed_hbm, seed_ref), (kappa_hbm, kappa_ref)))
    ]
    for load in loads + small:
        load.start()

    barrier = pltpu.get_barrier_semaphore()
    for i in range(1, Z):
        pl.semaphore_signal(barrier, inc=1, device_id=(lax.rem(z + i, Z) * 2 + core, g), device_id_type=MESH)
    for i in range(1, G):
        pl.semaphore_signal(barrier, inc=1, device_id=(c, lax.rem(g + i, G)), device_id_type=MESH)

    @pl.when(core == 0)
    def _():
        for i in range(Z):
            pl.semaphore_signal(barrier, inc=1, device_id=(lax.rem(z + i, Z) * 2 + 1, g), device_id_type=MESH)

    def send(phase, src, dst, device):
        pltpu.make_async_remote_copy(
            src_ref=src, dst_ref=dst, send_sem=send_sem.at[phase], recv_sem=recv_sem.at[phase],
            device_id=device, device_id_type=MESH,
        ).start()

    def wait_recv(phase, ref):
        pltpu.make_async_copy(ref, ref, recv_sem.at[phase]).wait()

    def wait_send(phase, ref):
        pltpu.make_async_copy(ref, ref, send_sem.at[phase]).wait()

    ncol = min(D, 256)

    def product(dst, dst_rows, lhs, rhs_ref, rhs_rows):
        @pl.loop(0, D // ncol)
        def _(j):
            cols = rows_at(j, ncol)
            dst[dst_rows, cols] = nn(lhs, rhs_ref[rhs_rows, cols]).astype(BF16)

    FAR = sorted(range(1, Z), key=lambda i: -min(i, Z - i))

    for i in range(chunks):
        loads[i].wait()
        at = pl.ds(i * rstep, rstep)
        v = x_ref[at, :].astype(F32)
        scale = lax.rsqrt(jnp.sum(v * v, axis=-1, keepdims=True) + EPSILON)
        rows[at, :] = (v * scale).astype(BF16)
    for load in small:
        load.wait()
    label = label_ref[...]
    member = member_ref[...]
    moving = label != c
    lz = lax.shift_right_logical(label, 1)
    side = label & 1
    own = pl.ds(0, R)

    hot[0:S, 0:R] = onehot(iota((S, R), 0) == jnp.where(moving & (side == 0), lz * G + member, -1))
    product(send_a, slice(None), hot[0:S, 0:R], rows, own)

    to_cluster = onehot((iota((128, R), 0) == label) & moving)
    to_member = onehot(iota((128, R), 0) == member)
    marks = nt(to_cluster, to_member)
    for i in range(C):
        mark_s[i] = marks[i:i + 1, :]
    mark_1[c] = mark_s[c]

    def cross_marks():
        for i in range(Z):
            tc = lax.rem(z + i, Z) * 2 + 1 - core
            send(4, mark_s.at[tc], mark_1.at[c], (tc, g))

    pl.semaphore_wait(barrier, Z - 1 + G - 1 + core * Z)
    for i in range(1, Z):
        tc = lax.rem(z + i, Z) * 2 + core
        send(2, mark_s.at[tc], mark_1.at[c], (tc, g))
    pl.when(core == 1)(cross_marks)

    @pl.when(core == 0)
    def _():
        for i in FAR:
            tz = lax.rem(z + i, Z)
            send(0, send_a.at[rows_at(tz, G)], mid_a.at[0, rows_at(z, G)], (tz * 2, g))
        mid_a[0, rows_at(z, G), :] = send_a[rows_at(z, G), :]

    @pl.when(core == 1)
    def _():
        for i in FAR + [0]:
            tz = lax.rem(z + i, Z)
            pl.semaphore_signal(ready, inc=1, device_id=(tz * 2, g), device_id_type=MESH)
            send(3, send_a.at[rows_at(tz, G)], mid_a.at[1, rows_at(z, G)], (tz * 2, g))

    n = round(G ** 0.5)
    hb = kb // 2
    Dh = D // 2
    px, py = g // n, lax.rem(g, n)
    first = (px, py)
    second = (py, px)
    ORDER = (2, 1, 3, 0)

    def at_plane(h, p, o):
        p, o = lax.rem(p + n, n), lax.rem(o + n, n)
        return p * n + o if h == 0 else o * n + p

    def block(h, dp, do):
        return at_plane(h, first[h] + dp, second[h] + do)

    def part_of(b, half=None):
        if half is None:
            return pl.ds(pl.multiple_of(b * kb, kb), kb)
        return pl.ds(pl.multiple_of(b * kb + half * hb, hb), hb)

    def push(phase, src, dst, sem, b):
        pltpu.make_async_remote_copy(
            src_ref=src, dst_ref=dst, send_sem=plane_send.at[phase], recv_sem=sem,
            device_id=(c, b), device_id_type=MESH,
        ).start()

    def landed(ref, sem):
        pltpu.make_async_copy(ref, ref, sem).wait()

    def sent(phase):
        for h in range(2):
            ref = part.at[h, pl.ds(0, (G - 1) * kb)]
            pltpu.make_async_copy(ref, ref, plane_send.at[phase]).wait()

    TOP, LOW = pl.ds(0, hb), pl.ds(hb, hb)

    def reduce_scatter(fill_far, fill_rest=None, meanwhile=None):
        for h in range(2):
            fill_far(h)
            ahead, behind = block(h, 1, 0), block(h, -1, 0)
            for r in ORDER:
                far = block(h, 2, r)
                push(0, part.at[h, part_of(far, 0)], relay.at[h, r, TOP], rs_sem.at[h, r, 0], ahead)
                push(0, part.at[h, part_of(far, 1)], relay.at[h, r, LOW], rs_sem.at[h, r, 1], behind)
        for h in range(2):
            if fill_rest is not None:
                fill_rest(h)
            ahead, behind = block(h, 1, 0), block(h, -1, 0)
            for r in ORDER:
                push(0, part.at[h, part_of(block(h, 1, r), 1)], nearer.at[h, r, 0, LOW], rs_sem.at[h, r, 2], ahead)
                push(0, part.at[h, part_of(block(h, -1, r), 0)], nearer.at[h, r, 1, TOP], rs_sem.at[h, r, 3], behind)
        if meanwhile is not None:
            meanwhile()
        for r in ORDER:
            for h in range(2):
                ahead, behind = block(h, 1, 0), block(h, -1, 0)
                landed(relay.at[h, r, TOP], rs_sem.at[h, r, 0])
                mine = part[h, part_of(block(h, 1, r), 0), :].astype(F32)
                combined[h, r, TOP, :] = (mine + relay[h, r, TOP, :].astype(F32)).astype(BF16)
                push(0, combined.at[h, r, TOP], nearer.at[h, r, 0, TOP], rs_sem.at[h, r, 4], ahead)
                landed(relay.at[h, r, LOW], rs_sem.at[h, r, 1])
                mine = part[h, part_of(block(h, -1, r), 1), :].astype(F32)
                combined[h, r, LOW, :] = (mine + relay[h, r, LOW, :].astype(F32)).astype(BF16)
                push(0, combined.at[h, r, LOW], nearer.at[h, r, 1, LOW], rs_sem.at[h, r, 5], behind)
        for r in ORDER:
            for h in range(2):
                landed(nearer.at[h, r, 0, LOW], rs_sem.at[h, r, 2])
                landed(nearer.at[h, r, 1, TOP], rs_sem.at[h, r, 3])
                landed(nearer.at[h, r, 0, TOP], rs_sem.at[h, r, 4])
                landed(nearer.at[h, r, 1, LOW], rs_sem.at[h, r, 5])
                total = part[h, part_of(block(h, 0, r)), :].astype(F32)
                total = total + nearer[h, r, 0].astype(F32) + nearer[h, r, 1].astype(F32)
                line[h, r] = total.astype(BF16)
                if r:
                    push(0, line.at[h, r], line_in.at[h, r - 1], rs_line_sem.at[h, r - 1], block(h, 0, r))
        totals = []
        for h in range(2):
            total = line[h, 0].astype(F32)
            for r in range(3):
                landed(line_in.at[h, r], rs_line_sem.at[h, r])
                total = total + line_in[h, r].astype(F32)
            totals.append(total)
        return totals

    def all_gather(blocks, meanwhile=None, midway=None):
        own_at = part_of(g)
        for h in range(2):
            centres[h, own_at, :] = blocks[h]

        def along(h, r):
            here = part_of(block(h, 0, r))
            push(1, centres.at[h, here], centres.at[h, here], ag_sem.at[h, r, 0], block(h, 1, 0))
            push(1, centres.at[h, here], centres.at[h, here], ag_sem.at[h, r, 1], block(h, -1, 0))
            if r == 2:
                push(1, centres.at[h, here], centres.at[h, here], ag_sem.at[h, r, 2], block(h, 2, 0))

        def forward(h, r):
            back, front = block(h, -1, r), block(h, 1, r)
            landed(centres.at[h, part_of(back)], ag_sem.at[h, r, 0])
            if r != 2:
                top = part_of(back, 0)
                push(1, centres.at[h, top], centres.at[h, top], ag_sem.at[h, r, 2], block(h, 1, 0))
            landed(centres.at[h, part_of(front)], ag_sem.at[h, r, 1])
            if r != 2:
                low = part_of(front, 1)
                push(1, centres.at[h, low], centres.at[h, low], ag_sem.at[h, r, 3], block(h, -1, 0))

        for h in range(2):
            for r in (1, 3, 2):
                push(1, centres.at[h, own_at], centres.at[h, own_at], ag_line_sem.at[h, r - 1], block(h, 0, r))
        for h in range(2):
            along(h, 0)
        if meanwhile is not None:
            meanwhile()
        for r in (3, 1):
            for h in range(2):
                landed(centres.at[h, part_of(block(h, 0, r))], ag_line_sem.at[h, n - r - 1])
                along(h, r)
        for h in range(2):
            forward(h, 0)
        for h in range(2):
            landed(centres.at[h, part_of(block(h, 0, 2))], ag_line_sem.at[h, 1])
            along(h, 2)
        if midway is not None:
            midway()
        for r in (3, 1, 2):
            for h in range(2):
                forward(h, r)
        for r in (0, 3, 1, 2):
            for h in range(2):
                far = block(h, 2, r)
                if r == 2:
                    landed(centres.at[h, part_of(far)], ag_sem.at[h, r, 2])
                else:
                    landed(centres.at[h, part_of(far, 0)], ag_sem.at[h, r, 2])
                    landed(centres.at[h, part_of(far, 1)], ag_sem.at[h, r, 3])

    hot[0:R, 0:K] = onehot(iota((R, K), 0) + g * R == seed_ref[...])
    hcol = min(Dh, 256)

    def fill_seeds(h):
        @pl.loop(0, Dh // hcol)
        def _(j):
            cols = pl.ds(pl.multiple_of(h * Dh + j * hcol, hcol), hcol)
            part[h, :, rows_at(j, hcol)] = tn(hot[0:R, 0:K], rows[own, cols]).astype(BF16)

    def fill_blocks(h, steps):
        targets = [part_of(block(h, dp, r)) for dp in steps for r in range(n)]
        lhs = jnp.concatenate([weights[at, :] for at in targets], axis=0)
        for j in range(Dh // hcol):
            sums = nn(lhs, rows[:, h * Dh + j * hcol:h * Dh + (j + 1) * hcol]).astype(BF16)
            for i, at in enumerate(targets):
                part[h, at, j * hcol:(j + 1) * hcol] = sums[i * kb:(i + 1) * kb, :]

    def other_rows():
        hot[0:S, 0:R] = onehot(iota((S, R), 0) == jnp.where(moving & (side == 1), member * Z + lz, -1))
        product(send_b, slice(None), hot[0:S, 0:R], rows, own)
        mid_b[rows_at(g, Z), :] = send_b[rows_at(g, Z), :]

    def other_sends():
        for i in range(1, G):
            tg = lax.rem(g + i, G)
            send(1, send_b.at[rows_at(tg, Z)], mid_b.at[rows_at(g, Z)], (c, tg))

        @pl.when(core == 0)
        def _():
            pl.semaphore_wait(ready, Z)
            cross_marks()

    landing = rows.at[pl.ds(pl.multiple_of(R + core * S + z * G, G), G)]

    def other_legs():
        turn_b = onehot((iota((S, S), 0) & (G - 1)) * Z + lax.div(iota((S, S), 0), G) == iota((S, S), 1))
        wait_recv(1, mid_b.at[pl.ds(0, S - Z)])
        product(fwd_b, slice(None), turn_b, mid_b, slice(None))

        @pl.when(core == 1)
        def _():
            for i in FAR:
                tz = lax.rem(z + i, Z)
                send(5, fwd_b.at[rows_at(tz, G)], landing, (tz * 2 + 1, g))
            landing[...] = fwd_b[rows_at(z, G), :]

        @pl.when(core == 0)
        def _():
            for i in FAR + [0]:
                tz = lax.rem(z + i, Z)
                send(6, fwd_b.at[rows_at(tz, G)], landing, (tz * 2 + 1, g))

    first_blocks = [t.astype(BF16) for t in reduce_scatter(fill_seeds, None, other_rows)]
    all_gather(first_blocks, other_sends, other_legs)
    sent(0)
    sent(1)

    wait_recv(2, mark_s.at[pl.ds(0, Z - 1)])
    wait_recv(4, mark_s.at[pl.ds(0, Z)])
    flat[...] = jnp.zeros_like(flat)
    for i in range(C):
        flat[i:i + 1, :] = mark_1[i]
    eye = onehot(iota((16, 128), 0) == iota((16, 128), 1))
    turned = nt(eye, flat[...].astype(BF16))
    for i in range(G):
        mark_2[i] = turned[i:i + 1, :]
    for i in range(1, G):
        tg = lax.rem(g + i, G)
        send(9, mark_2.at[tg], mark_3.at[g], (c, tg))
    mark_3[g] = mark_2[g]

    turn_a = onehot((iota((S, S), 0) & (Z - 1)) * G + lax.div(iota((S, S), 0), Z) == iota((S, S), 1))

    def second_leg(part_a, phase):
        at = pl.ds(pl.multiple_of(R + part_a * S + g * Z, Z), Z)

        @pl.loop(0, D // ncol)
        def _(j):
            cols = rows_at(j, ncol)
            fwd_a[part_a, :, cols] = nn(turn_a, mid_a[part_a, :, cols]).astype(BF16)

        for i in range(1, G):
            tg = lax.rem(g + i, G)
            send(phase, fwd_a.at[part_a, rows_at(tg, Z)], rows.at[at], (c, tg))
        rows[at, :] = fwd_a[part_a, rows_at(g, Z), :]

    @pl.when(core == 0)
    def _():
        wait_recv(0, mid_a.at[0, pl.ds(0, S - G)])
        second_leg(0, 8)
        wait_recv(3, mid_a.at[1])
        second_leg(1, 7)

    alive[:, 0:R] = jnp.where(moving, 0.0, 1.0)

    def origin(index):
        q = index & (S - 1)
        from_z = (1 - core) * (q & (Z - 1)) + core * lax.div(q, G)
        from_g = (1 - core) * lax.div(q, Z) + core * (q & (G - 1))
        return 2 * from_z + lax.div(index, S), from_g

    kappa = kappa_ref[0, 0]
    step = S

    def expectation(i):
        at = rows_at(i, step)
        scores = nt(centres[0], rows[at, 0:Dh]) + nt(centres[1], rows[at, Dh:D])
        scores = kappa * scores
        largest = jnp.max(scores, axis=0, keepdims=True)
        powered = jnp.exp(scores - largest)
        summed = jnp.sum(powered, axis=0, keepdims=True)
        here = alive[:, at]
        weights[:, at] = (powered * (1.0 / summed) * here).astype(BF16)
        norms[:, at] = (largest + jnp.log(summed)) * here

    own_steps = R // step
    pl.loop(0, own_steps)(expectation)

    wait_recv(9, mark_3.at[pl.ds(0, G - 1)])
    for i in range(G):
        flat[i:i + 1, :] = mark_3[i]
    from_c, from_g = origin(iota((1, 2 * S), 1))
    held = nn(flat[0:16, :].astype(BF16), onehot(iota((128, 2 * S), 0) == from_c))
    alive[:, R:] = jnp.sum(jnp.where(iota((16, 2 * S), 0) == from_g, held, 0.0), axis=0, keepdims=True)

    @pl.when(core == 0)
    def _():
        wait_recv(8, rows.at[pl.ds(0, S - Z)])

    @pl.when(core == 1)
    def _():
        wait_recv(5, rows.at[pl.ds(0, S - G)])

    expectation(own_steps + core)

    @pl.when(core == 0)
    def _():
        wait_recv(7, rows.at[pl.ds(0, S - Z)])

    @pl.when(core == 1)
    def _():
        wait_recv(6, rows.at[pl.ds(0, S)])

    expectation(own_steps + 1 - core)

    def place_scores():
        score_ref[:, 0:R] = norms[:, 0:R]
        from_c, from_g = origin(iota((2 * S, 1), 0))
        turn = onehot(iota((2 * S, 2 * S), 1) == from_c * G + from_g)
        moved = nn(split3(norms[:, R:]), turn)
        score_ref[:, R:] = moved[0:1, :] + moved[1:2, :] + moved[2:3, :]

    for it in range(ITERS):
        if it:
            for i in range(own_steps + 2):
                expectation(i)
        totals = reduce_scatter(lambda h: fill_blocks(h, (2,)), lambda h: fill_blocks(h, (1, 3, 0)))
        squares = [jnp.sum(t * t, axis=-1, keepdims=True) for t in totals]
        length = jnp.maximum(jnp.sqrt(squares[0] + squares[1]), 1.0)
        all_gather([(t / length).astype(BF16) for t in totals], place_scores if it == ITERS - 1 else None)
        sent(0)
        sent(1)
    cent_ref[:, 0:Dh] = centres[0]
    cent_ref[:, Dh:D] = centres[1]

    wait_send(1, send_b.at[pl.ds(0, S - Z)])
    wait_send(2, mark_s.at[pl.ds(0, Z - 1)])
    wait_send(4, mark_s.at[pl.ds(0, Z)])
    wait_send(9, mark_3.at[pl.ds(0, G - 1)])

    @pl.when(core == 0)
    def _():
        wait_send(0, send_a.at[pl.ds(0, S - G)])
        wait_send(6, rows.at[pl.ds(0, S)])
        wait_send(7, rows.at[pl.ds(0, S - Z)])
        wait_send(8, rows.at[pl.ds(0, S - Z)])

    @pl.when(core == 1)
    def _():
        wait_send(3, rows.at[pl.ds(0, S)])
        wait_send(5, rows.at[pl.ds(0, S - G)])


def shards(embeddings, new_label, dest_member, seed_index, kappa):
    R, D = embeddings.shape
    K = seed_index.shape[1]
    C = lax.axis_size("clusters")
    G = lax.axis_size("group")
    S = C * G // 2
    kb = K // G
    slots = R + 2 * S
    hbm = pl.BlockSpec(memory_space=pltpu.HBM)
    vmem = pl.BlockSpec(memory_space=pltpu.VMEM)
    phases = 10
    centroids, score = pl.pallas_call(
        functools.partial(kernel, (C, G, R, D, K)),
        name="refine",
        out_shape=(
            pltpu.VMEM((K, D), BF16),
            pltpu.VMEM((1, slots), F32),
        ),
        in_specs=[hbm] * 5,
        out_specs=(vmem, vmem),
        scratch_shapes=[
            pltpu.VMEM((R, D), BF16),
            pltpu.VMEM((1, R), I32),
            pltpu.VMEM((1, R), I32),
            pltpu.VMEM((1, K), I32),
            pltpu.SMEM((1, 1), F32),
            pltpu.VMEM((slots, D), BF16),
            pltpu.VMEM((max(R, K), max(R, K)), BF16),
            pltpu.VMEM((S, D), BF16),
            pltpu.VMEM((S, D), BF16),
            pltpu.VMEM((2, S, D), BF16),
            pltpu.VMEM((S, D), BF16),
            pltpu.VMEM((2, S, D), BF16),
            pltpu.VMEM((S, D), BF16),
            pltpu.VMEM((K, slots), BF16),
            pltpu.VMEM((2, K, D // 2), BF16),
            pltpu.VMEM((2, 4, kb, D // 2), BF16),
            pltpu.VMEM((2, 4, kb, D // 2), BF16),
            pltpu.VMEM((2, 4, 2, kb, D // 2), BF16),
            pltpu.VMEM((2, 4, kb, D // 2), BF16),
            pltpu.VMEM((2, 3, kb, D // 2), BF16),
            pltpu.VMEM((2, K, D // 2), BF16),
            pltpu.VMEM((1, slots), F32),
            pltpu.VMEM((1, slots), F32),
            pltpu.VMEM((C, 1, 128), F32),
            pltpu.VMEM((C, 1, 128), F32),
            pltpu.VMEM((G, 1, 128), F32),
            pltpu.VMEM((G, 1, 128), F32),
            pltpu.VMEM((128, 128), F32),
            pltpu.SemaphoreType.DMA((phases,)),
            pltpu.SemaphoreType.DMA((phases,)),
            pltpu.SemaphoreType.DMA((8,)),
            pltpu.SemaphoreType.REGULAR,
            pltpu.SemaphoreType.DMA((2,)),
            pltpu.SemaphoreType.DMA((2, 4, 6)),
            pltpu.SemaphoreType.DMA((2, 3)),
            pltpu.SemaphoreType.DMA((2, 4, 4)),
            pltpu.SemaphoreType.DMA((2, 3)),
        ],
        compiler_params=pltpu.CompilerParams(
            collective_id=0, has_side_effects=True, vmem_limit_bytes=60 * 1024 * 1024
        ),
    )(
        embeddings,
        new_label.reshape(1, R),
        dest_member.reshape(1, R),
        seed_index,
        kappa.reshape(1, 1),
    )
    return centroids, score.reshape(slots)


def solution(mesh):
    return jax.shard_map(
        shards,
        mesh=mesh,
        in_specs=(
            P(("clusters", "group"), None),
            P(("clusters", "group")),
            P(("clusters", "group")),
            P("clusters", None),
            P("clusters"),
        ),
        out_specs=(P("clusters", None), P(("clusters", "group"))),
        check_vma=False,
    )
```

```python
import functools

import jax
import jax.numpy as jnp
from jax import lax
from jax.experimental import pallas as pl
from jax.experimental.pallas import tpu as pltpu
from jax.sharding import PartitionSpec as P

ITERS = 2
EPSILON = 1e-06
MESH = pl.DeviceIdType.MESH
F32 = jnp.float32
BF16 = jnp.bfloat16
I32 = jnp.int32


def iota(shape, dim):
    return lax.broadcasted_iota(I32, shape, dim)


def onehot(cond):
    return jnp.where(cond, 1.0, 0.0).astype(BF16)


def nn(a, b):
    return lax.dot_general(a, b, (((1,), (0,)), ((), ())), preferred_element_type=F32)


def nt(a, b):
    return lax.dot_general(a, b, (((1,), (1,)), ((), ())), preferred_element_type=F32)


def tn(a, b):
    return lax.dot_general(a, b, (((0,), (0,)), ((), ())), preferred_element_type=F32)


def rows_at(index, size):
    if isinstance(index, int):
        return pl.ds(index * size, size)
    return pl.ds(pl.multiple_of(index * size, size), size)


def split3(v):
    hi = v.astype(BF16)
    rest = v - hi.astype(F32)
    mid = rest.astype(BF16)
    low = (rest - mid.astype(F32)).astype(BF16)
    pad = jnp.zeros((13,) + v.shape[1:], F32)
    return jnp.concatenate([hi.astype(F32), mid.astype(F32), low.astype(F32), pad], axis=0).astype(BF16)


def kernel(
    dims,
    x_hbm, label_hbm, member_hbm, seed_hbm, kappa_hbm,
    cent_ref, score_ref,
    x_ref, label_ref, member_ref, seed_ref, kappa_ref,
    rows, hot, send_a, send_b, mid_a, mid_b, fwd_a, fwd_b,
    weights, part, relay, combined, nearer, line, line_in, centres, alive, norms,
    mark_s, mark_1, mark_2, mark_3, flat,
    send_sem, recv_sem, load_sem, ready, plane_send, rs_sem, rs_line_sem, ag_sem, ag_line_sem,
):
    C, G, R, D, K = dims
    Z = C // 2
    S = Z * G
    kb = K // G
    c = lax.axis_index("clusters")
    g = lax.axis_index("group")
    z = c // 2
    core = lax.rem(c, 2)

    chunks = 4
    rstep = R // chunks
    loads = [
        pltpu.make_async_copy(x_hbm.at[pl.ds(i * rstep, rstep)], x_ref.at[pl.ds(i * rstep, rstep)], load_sem.at[4 + i])
        for i in range(chunks)
    ]
    small = [
        pltpu.make_async_copy(src, dst, load_sem.at[i])
        for i, (src, dst) in enumerate(((label_hbm, label_ref), (member_hbm, member_ref), (seed_hbm, seed_ref), (kappa_hbm, kappa_ref)))
    ]
    for load in loads + small:
        load.start()

    barrier = pltpu.get_barrier_semaphore()
    for i in range(1, Z):
        pl.semaphore_signal(barrier, inc=1, device_id=(lax.rem(z + i, Z) * 2 + core, g), device_id_type=MESH)
    for i in range(1, G):
        pl.semaphore_signal(barrier, inc=1, device_id=(c, lax.rem(g + i, G)), device_id_type=MESH)

    @pl.when(core == 0)
    def _():
        for i in range(Z):
            pl.semaphore_signal(barrier, inc=1, device_id=(lax.rem(z + i, Z) * 2 + 1, g), device_id_type=MESH)

    def send(phase, src, dst, device):
        pltpu.make_async_remote_copy(
            src_ref=src, dst_ref=dst, send_sem=send_sem.at[phase], recv_sem=recv_sem.at[phase],
            device_id=device, device_id_type=MESH,
        ).start()

    def wait_recv(phase, ref):
        pltpu.make_async_copy(ref, ref, recv_sem.at[phase]).wait()

    def wait_send(phase, ref):
        pltpu.make_async_copy(ref, ref, send_sem.at[phase]).wait()

    ncol = min(D, 256)

    def product(dst, dst_rows, lhs, rhs_ref, rhs_rows):
        @pl.loop(0, D // ncol)
        def _(j):
            cols = rows_at(j, ncol)
            dst[dst_rows, cols] = nn(lhs, rhs_ref[rhs_rows, cols]).astype(BF16)

    FAR = sorted(range(1, Z), key=lambda i: -min(i, Z - i))

    for i in range(chunks):
        loads[i].wait()
        at = pl.ds(i * rstep, rstep)
        v = x_ref[at, :].astype(F32)
        scale = lax.rsqrt(jnp.sum(v * v, axis=-1, keepdims=True) + EPSILON)
        rows[at, :] = (v * scale).astype(BF16)
    for load in small:
        load.wait()
    label = label_ref[...]
    member = member_ref[...]
    moving = label != c
    lz = lax.shift_right_logical(label, 1)
    side = label & 1
    own = pl.ds(0, R)

    hot[0:S, 0:R] = onehot(iota((S, R), 0) == jnp.where(moving & (side == 0), lz * G + member, -1))
    product(send_a, slice(None), hot[0:S, 0:R], rows, own)

    to_cluster = onehot((iota((128, R), 0) == label) & moving)
    to_member = onehot(iota((128, R), 0) == member)
    marks = nt(to_cluster, to_member)
    for i in range(C):
        mark_s[i] = marks[i:i + 1, :]
    mark_1[c] = mark_s[c]

    def cross_marks():
        for i in range(Z):
            tc = lax.rem(z + i, Z) * 2 + 1 - core
            send(4, mark_s.at[tc], mark_1.at[c], (tc, g))

    pl.semaphore_wait(barrier, Z - 1 + G - 1 + core * Z)
    for i in range(1, Z):
        tc = lax.rem(z + i, Z) * 2 + core
        send(2, mark_s.at[tc], mark_1.at[c], (tc, g))
    pl.when(core == 1)(cross_marks)

    @pl.when(core == 0)
    def _():
        for i in FAR:
            tz = lax.rem(z + i, Z)
            send(0, send_a.at[rows_at(tz, G)], mid_a.at[0, rows_at(z, G)], (tz * 2, g))
        mid_a[0, rows_at(z, G), :] = send_a[rows_at(z, G), :]

    @pl.when(core == 1)
    def _():
        for i in FAR + [0]:
            tz = lax.rem(z + i, Z)
            pl.semaphore_signal(ready, inc=1, device_id=(tz * 2, g), device_id_type=MESH)
            send(3, send_a.at[rows_at(tz, G)], mid_a.at[1, rows_at(z, G)], (tz * 2, g))

    n = round(G ** 0.5)
    hb = kb // 2
    Dh = D // 2
    px, py = g // n, lax.rem(g, n)
    first = (px, py)
    second = (py, px)
    ORDER = (2, 1, 3, 0)

    def at_plane(h, p, o):
        p, o = lax.rem(p + n, n), lax.rem(o + n, n)
        return p * n + o if h == 0 else o * n + p

    def block(h, dp, do):
        return at_plane(h, first[h] + dp, second[h] + do)

    def part_of(b, half=None):
        if half is None:
            return pl.ds(pl.multiple_of(b * kb, kb), kb)
        return pl.ds(pl.multiple_of(b * kb + half * hb, hb), hb)

    def push(phase, src, dst, sem, b):
        pltpu.make_async_remote_copy(
            src_ref=src, dst_ref=dst, send_sem=plane_send.at[phase], recv_sem=sem,
            device_id=(c, b), device_id_type=MESH,
        ).start()

    def landed(ref, sem):
        pltpu.make_async_copy(ref, ref, sem).wait()

    def sent(phase):
        for h in range(2):
            ref = part.at[h, pl.ds(0, (G - 1) * kb)]
            pltpu.make_async_copy(ref, ref, plane_send.at[phase]).wait()

    TOP, LOW = pl.ds(0, hb), pl.ds(hb, hb)

    def reduce_scatter(fill_far, fill_rest=None, meanwhile=None):
        for h in range(2):
            fill_far(h)
            ahead, behind = block(h, 1, 0), block(h, -1, 0)
            for r in ORDER:
                far = block(h, 2, r)
                if r == 2:
                    push(0, part.at[h, part_of(far)], relay.at[h, r], rs_sem.at[h, r, 0], block(h, 2, 0))
                    continue
                push(0, part.at[h, part_of(far, 0)], relay.at[h, r, TOP], rs_sem.at[h, r, 0], ahead)
                push(0, part.at[h, part_of(far, 1)], relay.at[h, r, LOW], rs_sem.at[h, r, 1], behind)
        for h in range(2):
            if fill_rest is not None:
                fill_rest(h)
            ahead, behind = block(h, 1, 0), block(h, -1, 0)
            for r in ORDER:
                if r == 2:
                    push(0, part.at[h, part_of(block(h, 1, r))], nearer.at[h, r, 0], rs_sem.at[h, r, 2], ahead)
                    push(0, part.at[h, part_of(block(h, -1, r))], nearer.at[h, r, 1], rs_sem.at[h, r, 3], behind)
                    continue
                push(0, part.at[h, part_of(block(h, 1, r), 1)], nearer.at[h, r, 0, LOW], rs_sem.at[h, r, 2], ahead)
                push(0, part.at[h, part_of(block(h, -1, r), 0)], nearer.at[h, r, 1, TOP], rs_sem.at[h, r, 3], behind)
        if meanwhile is not None:
            meanwhile()

        def relayed(r):
            for h in range(2):
                ahead, behind = block(h, 1, 0), block(h, -1, 0)
                landed(relay.at[h, r, TOP], rs_sem.at[h, r, 0])
                mine = part[h, part_of(block(h, 1, r), 0), :].astype(F32)
                combined[h, r, TOP, :] = (mine + relay[h, r, TOP, :].astype(F32)).astype(BF16)
                push(0, combined.at[h, r, TOP], nearer.at[h, r, 0, TOP], rs_sem.at[h, r, 4], ahead)
                landed(relay.at[h, r, LOW], rs_sem.at[h, r, 1])
                mine = part[h, part_of(block(h, -1, r), 1), :].astype(F32)
                combined[h, r, LOW, :] = (mine + relay[h, r, LOW, :].astype(F32)).astype(BF16)
                push(0, combined.at[h, r, LOW], nearer.at[h, r, 1, LOW], rs_sem.at[h, r, 5], behind)

        def along_line(r):
            for h in range(2):
                total = part[h, part_of(block(h, 0, r)), :].astype(F32)
                if r == 2:
                    landed(nearer.at[h, r, 0], rs_sem.at[h, r, 2])
                    landed(nearer.at[h, r, 1], rs_sem.at[h, r, 3])
                    landed(relay.at[h, r], rs_sem.at[h, r, 0])
                    total = total + relay[h, r].astype(F32)
                else:
                    landed(nearer.at[h, r, 0, LOW], rs_sem.at[h, r, 2])
                    landed(nearer.at[h, r, 1, TOP], rs_sem.at[h, r, 3])
                    landed(nearer.at[h, r, 0, TOP], rs_sem.at[h, r, 4])
                    landed(nearer.at[h, r, 1, LOW], rs_sem.at[h, r, 5])
                total = total + nearer[h, r, 0].astype(F32) + nearer[h, r, 1].astype(F32)
                line[h, r] = total.astype(BF16)
                if r:
                    push(0, line.at[h, r], line_in.at[h, r - 1], rs_line_sem.at[h, r - 1], block(h, 0, r))

        relayed(1)
        relayed(3)
        along_line(2)
        relayed(0)
        along_line(1)
        along_line(3)
        along_line(0)
        totals = []
        for h in range(2):
            total = line[h, 0].astype(F32)
            for r in range(3):
                landed(line_in.at[h, r], rs_line_sem.at[h, r])
                total = total + line_in[h, r].astype(F32)
            totals.append(total)
        return totals

    def all_gather(blocks, meanwhile=None, midway=None):
        own_at = part_of(g)
        for h in range(2):
            centres[h, own_at, :] = blocks[h]

        def along(h, r):
            here = part_of(block(h, 0, r))
            push(1, centres.at[h, here], centres.at[h, here], ag_sem.at[h, r, 0], block(h, 1, 0))
            push(1, centres.at[h, here], centres.at[h, here], ag_sem.at[h, r, 1], block(h, -1, 0))
            if r == 2:
                push(1, centres.at[h, here], centres.at[h, here], ag_sem.at[h, r, 2], block(h, 2, 0))

        def forward(h, r):
            back, front = block(h, -1, r), block(h, 1, r)
            landed(centres.at[h, part_of(back)], ag_sem.at[h, r, 0])
            if r != 2:
                top = part_of(back, 0)
                push(1, centres.at[h, top], centres.at[h, top], ag_sem.at[h, r, 2], block(h, 1, 0))
            landed(centres.at[h, part_of(front)], ag_sem.at[h, r, 1])
            if r != 2:
                low = part_of(front, 1)
                push(1, centres.at[h, low], centres.at[h, low], ag_sem.at[h, r, 3], block(h, -1, 0))

        for h in range(2):
            for r in (1, 3, 2):
                push(1, centres.at[h, own_at], centres.at[h, own_at], ag_line_sem.at[h, r - 1], block(h, 0, r))
        for h in range(2):
            along(h, 0)
        if meanwhile is not None:
            meanwhile()
        for r in (3, 1):
            for h in range(2):
                landed(centres.at[h, part_of(block(h, 0, r))], ag_line_sem.at[h, n - r - 1])
                along(h, r)
        for h in range(2):
            forward(h, 0)
        for h in range(2):
            landed(centres.at[h, part_of(block(h, 0, 2))], ag_line_sem.at[h, 1])
            along(h, 2)
        if midway is not None:
            midway()
        for r in (3, 1, 2):
            for h in range(2):
                forward(h, r)
        for r in (0, 3, 1, 2):
            for h in range(2):
                far = block(h, 2, r)
                if r == 2:
                    landed(centres.at[h, part_of(far)], ag_sem.at[h, r, 2])
                else:
                    landed(centres.at[h, part_of(far, 0)], ag_sem.at[h, r, 2])
                    landed(centres.at[h, part_of(far, 1)], ag_sem.at[h, r, 3])

    hot[0:R, 0:K] = onehot(iota((R, K), 0) + g * R == seed_ref[...])
    hcol = min(Dh, 256)

    def fill_seeds(h):
        @pl.loop(0, Dh // hcol)
        def _(j):
            cols = pl.ds(pl.multiple_of(h * Dh + j * hcol, hcol), hcol)
            part[h, :, rows_at(j, hcol)] = tn(hot[0:R, 0:K], rows[own, cols]).astype(BF16)

    def fill_blocks(h, steps):
        targets = [part_of(block(h, dp, r)) for dp in steps for r in range(n)]
        lhs = jnp.concatenate([weights[at, :] for at in targets], axis=0)
        for j in range(Dh // hcol):
            sums = nn(lhs, rows[:, h * Dh + j * hcol:h * Dh + (j + 1) * hcol]).astype(BF16)
            for i, at in enumerate(targets):
                part[h, at, j * hcol:(j + 1) * hcol] = sums[i * kb:(i + 1) * kb, :]

    def other_rows():
        hot[0:S, 0:R] = onehot(iota((S, R), 0) == jnp.where(moving & (side == 1), member * Z + lz, -1))
        product(send_b, slice(None), hot[0:S, 0:R], rows, own)
        mid_b[rows_at(g, Z), :] = send_b[rows_at(g, Z), :]

    def other_sends():
        for i in range(1, G):
            tg = lax.rem(g + i, G)
            send(1, send_b.at[rows_at(tg, Z)], mid_b.at[rows_at(g, Z)], (c, tg))

        @pl.when(core == 0)
        def _():
            pl.semaphore_wait(ready, Z)
            cross_marks()

    landing = rows.at[pl.ds(pl.multiple_of(R + core * S + z * G, G), G)]

    def other_legs():
        turn_b = onehot((iota((S, S), 0) & (G - 1)) * Z + lax.div(iota((S, S), 0), G) == iota((S, S), 1))
        wait_recv(1, mid_b.at[pl.ds(0, S - Z)])
        product(fwd_b, slice(None), turn_b, mid_b, slice(None))

        @pl.when(core == 1)
        def _():
            for i in FAR:
                tz = lax.rem(z + i, Z)
                send(5, fwd_b.at[rows_at(tz, G)], landing, (tz * 2 + 1, g))
            landing[...] = fwd_b[rows_at(z, G), :]

        @pl.when(core == 0)
        def _():
            for i in FAR + [0]:
                tz = lax.rem(z + i, Z)
                send(6, fwd_b.at[rows_at(tz, G)], landing, (tz * 2 + 1, g))

    first_blocks = [t.astype(BF16) for t in reduce_scatter(fill_seeds, None, other_rows)]
    all_gather(first_blocks, other_sends, other_legs)
    sent(0)
    sent(1)

    wait_recv(2, mark_s.at[pl.ds(0, Z - 1)])
    wait_recv(4, mark_s.at[pl.ds(0, Z)])
    flat[...] = jnp.zeros_like(flat)
    for i in range(C):
        flat[i:i + 1, :] = mark_1[i]
    eye = onehot(iota((16, 128), 0) == iota((16, 128), 1))
    turned = nt(eye, flat[...].astype(BF16))
    for i in range(G):
        mark_2[i] = turned[i:i + 1, :]
    for i in range(1, G):
        tg = lax.rem(g + i, G)
        send(9, mark_2.at[tg], mark_3.at[g], (c, tg))
    mark_3[g] = mark_2[g]

    turn_a = onehot((iota((S, S), 0) & (Z - 1)) * G + lax.div(iota((S, S), 0), Z) == iota((S, S), 1))

    def second_leg(part_a, phase):
        at = pl.ds(pl.multiple_of(R + part_a * S + g * Z, Z), Z)

        @pl.loop(0, D // ncol)
        def _(j):
            cols = rows_at(j, ncol)
            fwd_a[part_a, :, cols] = nn(turn_a, mid_a[part_a, :, cols]).astype(BF16)

        for i in range(1, G):
            tg = lax.rem(g + i, G)
            send(phase, fwd_a.at[part_a, rows_at(tg, Z)], rows.at[at], (c, tg))
        rows[at, :] = fwd_a[part_a, rows_at(g, Z), :]

    @pl.when(core == 0)
    def _():
        wait_recv(0, mid_a.at[0, pl.ds(0, S - G)])
        second_leg(0, 8)
        wait_recv(3, mid_a.at[1])
        second_leg(1, 7)

    alive[:, 0:R] = jnp.where(moving, 0.0, 1.0)

    def origin(index):
        q = index & (S - 1)
        from_z = (1 - core) * (q & (Z - 1)) + core * lax.div(q, G)
        from_g = (1 - core) * lax.div(q, Z) + core * (q & (G - 1))
        return 2 * from_z + lax.div(index, S), from_g

    kappa = kappa_ref[0, 0]
    step = S

    def expectation(i):
        at = rows_at(i, step)
        scores = nt(centres[0], rows[at, 0:Dh]) + nt(centres[1], rows[at, Dh:D])
        scores = kappa * scores
        largest = jnp.max(scores, axis=0, keepdims=True)
        powered = jnp.exp(scores - largest)
        summed = jnp.sum(powered, axis=0, keepdims=True)
        here = alive[:, at]
        weights[:, at] = (powered * (1.0 / summed) * here).astype(BF16)
        norms[:, at] = (largest + jnp.log(summed)) * here

    own_steps = R // step
    pl.loop(0, own_steps)(expectation)

    wait_recv(9, mark_3.at[pl.ds(0, G - 1)])
    for i in range(G):
        flat[i:i + 1, :] = mark_3[i]
    from_c, from_g = origin(iota((1, 2 * S), 1))
    held = nn(flat[0:16, :].astype(BF16), onehot(iota((128, 2 * S), 0) == from_c))
    alive[:, R:] = jnp.sum(jnp.where(iota((16, 2 * S), 0) == from_g, held, 0.0), axis=0, keepdims=True)

    @pl.when(core == 0)
    def _():
        wait_recv(8, rows.at[pl.ds(0, S - Z)])

    @pl.when(core == 1)
    def _():
        wait_recv(5, rows.at[pl.ds(0, S - G)])

    expectation(own_steps + core)

    @pl.when(core == 0)
    def _():
        wait_recv(7, rows.at[pl.ds(0, S - Z)])

    @pl.when(core == 1)
    def _():
        wait_recv(6, rows.at[pl.ds(0, S)])

    expectation(own_steps + 1 - core)

    def place_scores():
        score_ref[:, 0:R] = norms[:, 0:R]
        from_c, from_g = origin(iota((2 * S, 1), 0))
        turn = onehot(iota((2 * S, 2 * S), 1) == from_c * G + from_g)
        moved = nn(split3(norms[:, R:]), turn)
        score_ref[:, R:] = moved[0:1, :] + moved[1:2, :] + moved[2:3, :]

    for it in range(ITERS):
        if it:
            for i in range(own_steps + 2):
                expectation(i)
        totals = reduce_scatter(lambda h: fill_blocks(h, (2,)), lambda h: fill_blocks(h, (1, 3, 0)))
        squares = [jnp.sum(t * t, axis=-1, keepdims=True) for t in totals]
        length = jnp.maximum(jnp.sqrt(squares[0] + squares[1]), 1.0)
        all_gather([(t / length).astype(BF16) for t in totals], place_scores if it == ITERS - 1 else None)
        sent(0)
        sent(1)
    cent_ref[:, 0:Dh] = centres[0]
    cent_ref[:, Dh:D] = centres[1]

    wait_send(1, send_b.at[pl.ds(0, S - Z)])
    wait_send(2, mark_s.at[pl.ds(0, Z - 1)])
    wait_send(4, mark_s.at[pl.ds(0, Z)])
    wait_send(9, mark_3.at[pl.ds(0, G - 1)])

    @pl.when(core == 0)
    def _():
        wait_send(0, send_a.at[pl.ds(0, S - G)])
        wait_send(6, rows.at[pl.ds(0, S)])
        wait_send(7, rows.at[pl.ds(0, S - Z)])
        wait_send(8, rows.at[pl.ds(0, S - Z)])

    @pl.when(core == 1)
    def _():
        wait_send(3, rows.at[pl.ds(0, S)])
        wait_send(5, rows.at[pl.ds(0, S - G)])


def shards(embeddings, new_label, dest_member, seed_index, kappa):
    R, D = embeddings.shape
    K = seed_index.shape[1]
    C = lax.axis_size("clusters")
    G = lax.axis_size("group")
    S = C * G // 2
    kb = K // G
    slots = R + 2 * S
    hbm = pl.BlockSpec(memory_space=pltpu.HBM)
    vmem = pl.BlockSpec(memory_space=pltpu.VMEM)
    phases = 10
    centroids, score = pl.pallas_call(
        functools.partial(kernel, (C, G, R, D, K)),
        name="refine",
        out_shape=(
            pltpu.VMEM((K, D), BF16),
            pltpu.VMEM((1, slots), F32),
        ),
        in_specs=[hbm] * 5,
        out_specs=(vmem, vmem),
        scratch_shapes=[
            pltpu.VMEM((R, D), BF16),
            pltpu.VMEM((1, R), I32),
            pltpu.VMEM((1, R), I32),
            pltpu.VMEM((1, K), I32),
            pltpu.SMEM((1, 1), F32),
            pltpu.VMEM((slots, D), BF16),
            pltpu.VMEM((max(R, K), max(R, K)), BF16),
            pltpu.VMEM((S, D), BF16),
            pltpu.VMEM((S, D), BF16),
            pltpu.VMEM((2, S, D), BF16),
            pltpu.VMEM((S, D), BF16),
            pltpu.VMEM((2, S, D), BF16),
            pltpu.VMEM((S, D), BF16),
            pltpu.VMEM((K, slots), BF16),
            pltpu.VMEM((2, K, D // 2), BF16),
            pltpu.VMEM((2, 4, kb, D // 2), BF16),
            pltpu.VMEM((2, 4, kb, D // 2), BF16),
            pltpu.VMEM((2, 4, 2, kb, D // 2), BF16),
            pltpu.VMEM((2, 4, kb, D // 2), BF16),
            pltpu.VMEM((2, 3, kb, D // 2), BF16),
            pltpu.VMEM((2, K, D // 2), BF16),
            pltpu.VMEM((1, slots), F32),
            pltpu.VMEM((1, slots), F32),
            pltpu.VMEM((C, 1, 128), F32),
            pltpu.VMEM((C, 1, 128), F32),
            pltpu.VMEM((G, 1, 128), F32),
            pltpu.VMEM((G, 1, 128), F32),
            pltpu.VMEM((128, 128), F32),
            pltpu.SemaphoreType.DMA((phases,)),
            pltpu.SemaphoreType.DMA((phases,)),
            pltpu.SemaphoreType.DMA((8,)),
            pltpu.SemaphoreType.REGULAR,
            pltpu.SemaphoreType.DMA((2,)),
            pltpu.SemaphoreType.DMA((2, 4, 6)),
            pltpu.SemaphoreType.DMA((2, 3)),
            pltpu.SemaphoreType.DMA((2, 4, 4)),
            pltpu.SemaphoreType.DMA((2, 3)),
        ],
        compiler_params=pltpu.CompilerParams(
            collective_id=0, has_side_effects=True, vmem_limit_bytes=60 * 1024 * 1024
        ),
    )(
        embeddings,
        new_label.reshape(1, R),
        dest_member.reshape(1, R),
        seed_index,
        kappa.reshape(1, 1),
    )
    return centroids, score.reshape(slots)


def solution(mesh):
    return jax.shard_map(
        shards,
        mesh=mesh,
        in_specs=(
            P(("clusters", "group"), None),
            P(("clusters", "group")),
            P(("clusters", "group")),
            P("clusters", None),
            P("clusters"),
        ),
        out_specs=(P("clusters", None), P(("clusters", "group"))),
        check_vma=False,
    )
```
